32 devices in a mesh: ctx: 16 (over z, y, core), ch: 2 (over x).
Axes of the slice: x: 2, y: 2, z: 4, core: 2. Of those that a mesh axis runs over, the one named last changes fastest.
Arguments:
- query_proj: bfloat16 [2048, 8192], P('ctx', 'ch'), may hold values from -31 to 31
- key_proj: bfloat16 [2048, 8192], P('ctx', 'ch'), may hold values from -6 to 6
- value_proj: bfloat16 [2048, 8192], P('ctx', 'ch'), may hold values from -6 to 6
- key_taps: bfloat16 [512, 3], P('ch'), may hold values from -3.5 to 3.5
- value_taps: bfloat16 [512, 3], P('ch'), may hold values from -3.5 to 3.5
- residues: float32 [512, 16], P('ch'), may hold values from -0.06 to 0.06
- decay_rates: float32 [512, 16], P('ch'), may hold values from 5e-06 to 0.05
- skip_weight: float32 [8192], P('ch'), may hold values from 0.5 to 1.5
- norm_gain: float32 [8192], P('ch'), may hold values from 0.5 to 1.5
- out_grad: bfloat16 [2048, 8192], P('ctx', 'ch'), may hold values from -6 to 6
Outputs:
- mixed_out: bfloat16 [2048, 8192], P('ctx', 'ch')
- query_grad: bfloat16 [2048, 8192], P('ctx', 'ch')
- key_grad: bfloat16 [2048, 8192], P('ctx', 'ch')
- value_grad: bfloat16 [2048, 8192], P('ctx', 'ch')
- key_taps_grad: float32 [512, 3], P('ch')
- value_taps_grad: float32 [512, 3], P('ch')
- skip_grad: float32 [8192], P('ch')
- gain_grad: float32 [8192], P('ch')
The draws below stay inside these ranges and needn't reach their ends.
All inputs are finite; a program needn't handle non-finite values.
Results may differ from the reference program's by a relative error of at most 0.006.
Values may be sent and summed in bfloat16 or wider, within the bound.
A program may use at most 128 MiB of HBM per device.

```python
import jax
import jax.numpy as jnp
from jax import lax

D = 8192
ORDER = 3
MODES = 16
TOKENS = 2048
GROUPS = 512


def draw_query_proj(key, part):
    column = jnp.arange(D).astype(jnp.float32) / D
    rising = jnp.exp(jnp.log(3.0) * column)
    values = jnp.clip(jax.random.normal(key, (TOKENS, D), jnp.float32), -6.0, 6.0) * rising
    return values.astype(jnp.bfloat16)


def mode_kinds(key):
    bits = jax.random.randint(jax.random.fold_in(key, 7001), (GROUPS, MODES), 0, 2)
    return bits == 1


def draw_decay_rates(key, part):
    quick = mode_kinds(key)
    key_fast, key_slow = jax.random.split(jax.random.fold_in(key, 7002))
    fast_rates = jnp.exp(jax.random.uniform(key_fast, (GROUPS, MODES), jnp.float32, jnp.log(0.01), jnp.log(0.05)))
    slow_rates = jnp.exp(jax.random.uniform(key_slow, (GROUPS, MODES), jnp.float32, jnp.log(5e-06), jnp.log(0.0002)))
    rates = jnp.where(quick, fast_rates, slow_rates)
    return jnp.clip(rates, 5e-06, 0.05).astype(jnp.float32)


def draw_residues(key, part):
    quick = mode_kinds(key)
    key_sign, key_fast, key_slow = jax.random.split(jax.random.fold_in(key, 7003), 3)
    signs = (2 * jax.random.randint(key_sign, (GROUPS, 1), 0, 2) - 1).astype(jnp.float32)
    fast_size = jax.random.uniform(key_fast, (GROUPS, MODES), jnp.float32, 0.03, 0.06)
    slow_size = jax.random.uniform(key_slow, (GROUPS, MODES), jnp.float32, 0.002, 0.008)
    values = signs * jnp.where(quick, fast_size, slow_size)
    return jnp.clip(values, -0.06, 0.06).astype(jnp.float32)


def levels(key, extent, pieces, smallest, high):
    factor_of, own = 1.0, jax.random.fold_in(key, 6)
    for position, parts in pieces:
        heights = jnp.exp(jax.random.uniform(jax.random.fold_in(own, position), (parts,), jnp.float32, smallest / len(pieces), high / len(pieces)))
        factor_of = factor_of * jnp.repeat(heights, extent[position] // parts).reshape([-1 if axis == position else 1 for axis in range(len(extent))])
    return factor_of


def centred(stream_key, dims, scale, limit, pieces=(), dtype=jnp.bfloat16):
    entries = jax.random.normal(stream_key, dims, jnp.float32) * scale
    if len(pieces) > 0:
        entries = levels(stream_key, dims, pieces, -0.22, 0.18) * entries
    return jnp.clip(entries, min=-limit, max=limit).astype(dtype)


def setup_inputs(seed: int = 0) -> dict:
    key_of = jax.random.split(jax.random.key(seed), 11)
    return {
        "query_proj": draw_query_proj(jax.random.fold_in(key_of[10], 71), 0),
        "key_proj": centred(key_of[1], (TOKENS, D), 1.0, 6.0, ((0, 16), (1, 2))),
        "value_proj": centred(key_of[2], (TOKENS, D), 1.0, 6.0, ((0, 16), (1, 2))),
        "key_taps": centred(key_of[3], (GROUPS, ORDER), ORDER ** -0.5, 3.5, ((0, 2),)),
        "value_taps": centred(key_of[4], (GROUPS, ORDER), ORDER ** -0.5, 3.5, ((0, 2),)),
        "residues": draw_residues(jax.random.fold_in(key_of[10], 71), 0),
        "decay_rates": draw_decay_rates(jax.random.fold_in(key_of[10], 71), 0),
        "skip_weight": jnp.clip(0.5 + 1.0 * jax.random.uniform(key_of[7], (D,), jnp.float32) ** levels(key_of[7], (D,), ((0, 2),), -0.2, 0.2), 0.5, 1.5),
        "norm_gain": jnp.clip(1.0 + 0.1 * jax.random.normal(key_of[8], (D,), jnp.float32), 0.5, 1.5),
        "out_grad": centred(key_of[9], (TOKENS, D), 1.0, 6.0, ((0, 16), (1, 2))),
    }


EPSILON = 1e-06

def decay_filter(residues, decay_rates, length):
    lagged = jnp.arange(length).astype(jnp.float32)
    return lax.optimization_barrier(jnp.sum(residues[:, :, None] * jnp.exp(-decay_rates[:, :, None] * lagged[None, None, :]), axis=1))

def spread_groups(table, width):
    return jnp.repeat(table, width // table.shape[0], axis=0)

def short_conv(signal, taps):
    tap_count = taps.shape[1]
    length, width = signal.shape
    padded = jnp.concatenate([jnp.zeros((tap_count - 1, width), jnp.float32), signal.astype(jnp.float32)], 0)
    spread = spread_groups(taps.astype(jnp.float32), width)

    def add_tap(offset, accum):
        begin = (tap_count - 1 - offset).astype(jnp.int32)
        window = lax.dynamic_slice_in_dim(padded, begin, length, 0)
        column = lax.dynamic_index_in_dim(spread, offset.astype(jnp.int32), 1, keepdims=False)
        return accum + window * column[None, :]
    return lax.fori_loop(0, tap_count, add_tap, jnp.zeros((length, width), jnp.float32))

def short_adjoint(grad_rows, taps):
    tap_count = taps.shape[1]
    length, width = grad_rows.shape
    padded = jnp.concatenate([grad_rows.astype(jnp.float32), jnp.zeros((tap_count - 1, width), jnp.float32)], 0)
    spread = spread_groups(taps.astype(jnp.float32), width)

    def add_tap(offset, accum):
        window = lax.dynamic_slice_in_dim(padded, offset.astype(jnp.int32), length, 0)
        column = lax.dynamic_index_in_dim(spread, offset.astype(jnp.int32), 1, keepdims=False)
        return accum + window * column[None, :]
    return lax.fori_loop(0, tap_count, add_tap, jnp.zeros((length, width), jnp.float32))

def taps_gradient(grad_rows, signal, groups, tap_count):
    length, width = signal.shape
    padded = jnp.concatenate([jnp.zeros((tap_count - 1, width), jnp.float32), signal.astype(jnp.float32)], 0)
    grad_wide = grad_rows.astype(jnp.float32)

    def one_tap(offset):
        begin = (tap_count - 1 - offset).astype(jnp.int32)
        window = lax.dynamic_slice_in_dim(padded, begin, length, 0)
        per_channel = lax.optimization_barrier(jnp.sum(grad_wide * window, axis=0))
        return lax.optimization_barrier(jnp.sum(per_channel.reshape(groups, width // groups), axis=1))
    return lax.map(one_tap, jnp.arange(tap_count).astype(jnp.int32)).T

def causal_long(signal, filt):
    length = signal.shape[0]
    spectrum = jnp.fft.rfft(signal, n=2 * length, axis=0)
    kernel = jnp.fft.rfft(filt, n=2 * length, axis=1)
    kernel = spread_groups(kernel, signal.shape[1]).T
    return jnp.fft.irfft(spectrum * kernel, n=2 * length, axis=0)[:length]

def reference(query_proj, key_proj, value_proj, key_taps, value_taps, residues, decay_rates, skip_weight, norm_gain, out_grad):
    groups, tap_count = key_taps.shape
    width = key_proj.shape[1]
    length = key_proj.shape[0]
    key_mixed = short_conv(key_proj, key_taps)
    value_mixed = short_conv(value_proj, value_taps)
    product = (key_mixed * value_mixed).astype(jnp.bfloat16)
    filt = decay_filter(residues, decay_rates, length)
    product_wide = product.astype(jnp.float32)
    mixed = causal_long(product_wide, filt) + skip_weight[None, :] * product_wide
    query_wide = query_proj.astype(jnp.float32)
    gated = query_wide * mixed
    squares = lax.optimization_barrier(jnp.sum(gated * gated, axis=1))
    scaled = lax.rsqrt(squares / width + EPSILON)[:, None]
    mixed_out = (gated * scaled * norm_gain).astype(jnp.bfloat16)
    grad_wide = out_grad.astype(jnp.float32)
    projected = lax.optimization_barrier(jnp.sum(gated * norm_gain * grad_wide, axis=1))
    gated_grad = scaled * norm_gain * grad_wide - gated * (scaled * scaled * scaled * projected[:, None] / width)
    gain_grad = lax.optimization_barrier(jnp.sum(grad_wide * gated * scaled, axis=0))
    query_grad = (gated_grad * mixed).astype(jnp.bfloat16)
    mixed_grad = (gated_grad * query_wide).astype(jnp.bfloat16)
    mixed_grad_wide = mixed_grad.astype(jnp.float32)
    backward_long = jnp.flip(causal_long(jnp.flip(mixed_grad_wide, 0), filt), 0)
    product_grad = backward_long + skip_weight[None, :] * mixed_grad_wide
    skip_grad = lax.optimization_barrier(jnp.sum(mixed_grad_wide * product_wide, axis=0))
    key_mixed_grad = (product_grad * value_mixed).astype(jnp.bfloat16)
    value_mixed_grad = (product_grad * key_mixed).astype(jnp.bfloat16)
    key_grad = short_adjoint(key_mixed_grad, key_taps).astype(jnp.bfloat16)
    value_grad = short_adjoint(value_mixed_grad, value_taps).astype(jnp.bfloat16)
    key_taps_grad = taps_gradient(key_mixed_grad, key_proj, groups, tap_count)
    value_taps_grad = taps_gradient(value_mixed_grad, value_proj, groups, tap_count)
    return (mixed_out, query_grad, key_grad, value_grad, key_taps_grad, value_taps_grad, skip_grad, gain_grad)
```

```python
import functools

import jax
import jax.numpy as jnp
from jax import lax
from jax.experimental import pallas as pl
from jax.experimental.pallas import tpu as pltpu
from jax.sharding import PartitionSpec as P

EPSILON = 1e-06
TILE = 256
F32, BF16 = jnp.float32, jnp.bfloat16


def halves(wide):
    high = wide.astype(BF16)
    return high, (wide - high.astype(F32)).astype(BF16)


def contract_rows(weights, signal):
    return lax.dot_general(weights, signal, (((0,), (0,)), ((), ())), preferred_element_type=F32)


def body(
    n, n_ch, slices, width_all, group_size,
    q_ref, k_ref, v_ref, og_ref, prm_ref, rate_ref, filt_ref, turned_ref,
    out_ref, qg_ref, kg_ref, vg_ref, sum_ref,
    tail_out, tail_in, head_out, head_in,
    prod, kmix, vmix, mixed, mgrad, kmg, vmg,
    own, gathered, prefix, incoming,
    own_b, gathered_b, suffix, incoming_b,
    part, parts, total,
    row_acc, row_out, row_in,
    tail_sem, head_sem, send_sem, recv_sem, ch_send, ch_recv,
):
    me = lax.axis_index("ctx")
    me_ch = lax.axis_index("ch")
    rows = q_ref.shape[0]

    def to_ctx(src, dst, s_sem, r_sem, peer):
        return pltpu.make_async_remote_copy(
            src_ref=src, dst_ref=dst, send_sem=s_sem, recv_sem=r_sem,
            device_id={"ctx": peer}, device_id_type=pl.DeviceIdType.MESH,
        )

    def columns(j):
        return pl.ds(pl.multiple_of(j * TILE, TILE), TILE)

    barrier = pltpu.get_barrier_semaphore()

    @pl.loop(1, n)
    def _(i):
        pl.semaphore_signal(
            barrier, inc=1, device_id={"ctx": lax.rem(me + i, n)},
            device_id_type=pl.DeviceIdType.MESH,
        )

    for i in range(1, n_ch):
        pl.semaphore_signal(
            barrier, inc=1, device_id={"ch": lax.rem(me_ch + i, n_ch)},
            device_id_type=pl.DeviceIdType.MESH,
        )
    tail_out[0:2] = k_ref[rows - 16 : rows].astype(F32)[14:16]
    tail_out[2:4] = v_ref[rows - 16 : rows].astype(F32)[14:16]
    pl.semaphore_wait(barrier, n - 1 + n_ch - 1)

    tails = to_ctx(tail_out, tail_in, tail_sem.at[0], tail_sem.at[1], lax.rem(me + 1, n))
    heads = to_ctx(head_out, head_in, head_sem.at[0], head_sem.at[1], lax.rem(me + n - 1, n))

    @pl.when(me < n - 1)
    def _():
        tails.start()

    @pl.when(me == 0)
    def _():
        tail_in[...] = jnp.zeros(tail_in.shape, F32)

    @pl.when(me > 0)
    def _():
        tails.wait_recv()

    row = lax.broadcasted_iota(jnp.int32, (rows, TILE), 0)
    row_wide = row.astype(F32)
    lane_group = lax.broadcasted_iota(jnp.int32, (rows, TILE), 1) // group_size
    block_mask = (
        lax.broadcasted_iota(jnp.int32, (TILE, TILE), 0) // group_size
        == lax.broadcasted_iota(jnp.int32, (TILE, TILE), 1) // group_size
    )
    tri_row = lax.broadcasted_iota(jnp.int32, (rows, rows), 0)
    tri_col = lax.broadcasted_iota(jnp.int32, (rows, rows), 1)
    groups_tile = TILE // group_size

    def delayed(ref, cols, base):
        wide = ref[:, cols].astype(F32)
        older = tail_in[base : base + 1, cols]
        newer = tail_in[base + 1 : base + 2, cols]
        one = jnp.where(row == 0, newer, pltpu.roll(wide, 1, 0))
        two = jnp.where(row == 0, older, jnp.where(row == 1, newer, pltpu.roll(wide, 2, 0)))
        return wide, one, two

    def modal(weights, signal):
        high, low = halves(weights)
        full = contract_rows(
            jnp.concatenate([high, low], axis=0), jnp.concatenate([signal, signal], axis=0)
        )
        kept = jnp.where(block_mask, full, 0.0)
        return jnp.sum(kept.reshape(groups_tile, group_size, TILE), axis=0)

    def spread(weights, state):
        high, low = halves(weights)
        tiled = jnp.where(block_mask, jnp.concatenate([state] * groups_tile, axis=0), 0.0)
        s_high, s_low = halves(tiled)
        return jnp.dot(
            jnp.concatenate([high, low, high], axis=1),
            jnp.concatenate([s_high, s_high, s_low], axis=0),
            preferred_element_type=F32,
        )

    def toeplitz(table, j, signal, keep):
        lines = table[pl.ds(pl.multiple_of(j * groups_tile, groups_tile), groups_tile), :]
        wide = signal.astype(F32)
        lhs, rhs = [], []
        for g in range(groups_tile):
            spread_line = jnp.broadcast_to(lines[g : g + 1, :], (rows, rows))
            turned = pltpu.roll(spread_line, 0, 1, stride=1, stride_axis=0)
            lhs.append(jnp.where(keep, turned, 0.0).astype(BF16))
            rhs.append(jnp.where(lane_group == g, wide, 0.0).astype(BF16))
        return jnp.dot(
            jnp.concatenate(lhs, axis=1), jnp.concatenate(rhs, axis=0),
            preferred_element_type=F32,
        )

    def scatter(phase, source, target, j):
        copy = to_ctx(
            source.at[j], target.at[me], send_sem.at[phase, j], recv_sem.at[phase, me], j
        )

        @pl.when(j != me)
        def _():
            copy.start()

        @pl.when(j == me)
        def _():
            target[me] = source[j]

    def arrive(phase, source, target, i):
        @pl.when(i != me)
        def _():
            to_ctx(
                source.at[0], target.at[i], send_sem.at[phase, 0], recv_sem.at[phase, i], i
            ).wait_recv()

    def sent(phase, source, target, count):
        @pl.loop(0, count)
        def _(j):
            @pl.when(j != me)
            def _():
                to_ctx(
                    source.at[j], target.at[me], send_sem.at[phase, j], recv_sem.at[phase, me], j
                ).wait_send()

    @pl.loop(0, slices)
    def _(i):
        j = lax.rem(me + i, slices)
        cols = columns(j)
        k0, k1, k2 = delayed(k_ref, cols, 0)
        key = k0 * prm_ref[0:1, cols] + k1 * prm_ref[1:2, cols] + k2 * prm_ref[2:3, cols]
        v0, v1, v2 = delayed(v_ref, cols, 2)
        value = v0 * prm_ref[3:4, cols] + v1 * prm_ref[4:5, cols] + v2 * prm_ref[5:6, cols]
        kmix[:, cols] = key
        vmix[:, cols] = value
        product = (key * value).astype(BF16)
        prod[:, cols] = product
        own[j] = modal(jnp.exp(-prm_ref[8:9, cols] * (rows - 1.0 - row_wide)), product)
        scatter(0, own, gathered, j)

    def long_forward(j):
        cols = columns(j)
        product = prod[:, cols]
        mixed[:, cols] = (
            toeplitz(turned_ref, j, product, tri_row >= tri_col)
            + prm_ref[6:7, cols] * product.astype(F32)
        )

    early = slices // 2

    @pl.loop(0, early)
    def _(j):
        long_forward(j)

    @pl.when(me < slices)
    def _():
        fall = jnp.exp(-rate_ref[:, columns(me)] * float(rows))

        def step(i, carry):
            prefix[i] = carry
            scatter(1, prefix, incoming, i)
            arrive(0, own, gathered, i)
            return fall * carry + gathered[i]

        lax.fori_loop(0, n, step, jnp.zeros((group_size, TILE), F32))

    @pl.loop(early, slices)
    def _(j):
        long_forward(j)

    row_acc[...] = jnp.zeros(row_acc.shape, F32)

    @pl.loop(0, slices)
    def _(i):
        j = lax.rem(me + i, slices)
        cols = columns(j)
        arrive(1, prefix, incoming, j)
        enter = prm_ref[9:10, cols] * jnp.exp(-prm_ref[8:9, cols] * (row_wide + 1.0))
        full = mixed[:, cols] + spread(enter, incoming[j])
        mixed[:, cols] = full
        gated = q_ref[:, cols].astype(F32) * full
        squares = gated * gated
        along = gated * prm_ref[7:8, cols] * og_ref[:, cols].astype(F32)
        row_acc[0] += squares[:, :128] + squares[:, 128:]
        row_acc[1] += along[:, :128] + along[:, 128:]

    lane = lax.broadcasted_iota(jnp.int32, (rows, 128), 1)
    squares = jnp.sum(row_acc[0], axis=1, keepdims=True)
    along = jnp.sum(row_acc[1], axis=1, keepdims=True)
    row_out[...] = jnp.where(lane == 0, squares, along)

    def to_ch(i):
        return pltpu.make_async_remote_copy(
            src_ref=row_out, dst_ref=row_in.at[i - 1], send_sem=ch_send.at[i - 1],
            recv_sem=ch_recv.at[i - 1], device_id={"ch": lax.rem(me_ch + i, n_ch)},
            device_id_type=pl.DeviceIdType.MESH,
        )

    for i in range(1, n_ch):
        to_ch(i).start()
    summed = row_out[...]
    for i in range(1, n_ch):
        to_ch(i).wait_recv()
        summed = summed + row_in[i - 1]
    squares, along = summed[:, 0:1], summed[:, 1:2]
    scaled = lax.rsqrt(squares / width_all + EPSILON)
    pull = scaled * scaled * scaled * along / width_all

    @pl.loop(0, slices)
    def _(i):
        j = lax.rem(me + i, slices)
        cols = columns(j)
        gain = prm_ref[7:8, cols]
        query = q_ref[:, cols].astype(F32)
        grad = og_ref[:, cols].astype(F32)
        full = mixed[:, cols]
        normed = query * full * scaled
        out_ref[:, cols] = (normed * gain).astype(BF16)
        gated_grad = scaled * gain * grad - query * full * pull
        qg_ref[:, cols] = (gated_grad * full).astype(BF16)
        mixed_grad = (gated_grad * query).astype(BF16)
        mgrad[:, cols] = mixed_grad
        mixed_wide = mixed_grad.astype(F32)
        part[j, 0:1, :] = jnp.sum(mixed_wide * prod[:, cols].astype(F32), axis=0, keepdims=True)
        part[j, 1:2, :] = jnp.sum(grad * normed, axis=0, keepdims=True)
        own_b[j] = modal(jnp.exp(-prm_ref[8:9, cols] * row_wide), mixed_grad)
        scatter(2, own_b, gathered_b, j)

    def long_backward(j):
        cols = columns(j)
        grad = mgrad[:, cols]
        mixed[:, cols] = (
            toeplitz(filt_ref, j, grad, tri_row <= tri_col)
            + prm_ref[6:7, cols] * grad.astype(F32)
        )

    @pl.loop(0, early)
    def _(j):
        long_backward(j)

    @pl.when(me < slices)
    def _():
        fall = jnp.exp(-rate_ref[:, columns(me)] * float(rows))

        def step(i, carry):
            place = n - 1 - i
            suffix[place] = carry
            scatter(3, suffix, incoming_b, place)
            arrive(2, own_b, gathered_b, place)
            return fall * carry + gathered_b[place]

        lax.fori_loop(0, n, step, jnp.zeros((group_size, TILE), F32))

    @pl.loop(early, slices)
    def _(j):
        long_backward(j)

    @pl.loop(0, slices)
    def _(i):
        j = lax.rem(me + i, slices)
        cols = columns(j)
        arrive(3, suffix, incoming_b, j)
        leave = prm_ref[9:10, cols] * jnp.exp(-prm_ref[8:9, cols] * (rows - row_wide))
        pgrad = mixed[:, cols] + spread(leave, incoming_b[j])
        key_grad = (pgrad * vmix[:, cols]).astype(BF16)
        value_grad = (pgrad * kmix[:, cols]).astype(BF16)
        kmg[:, cols] = key_grad
        vmg[:, cols] = value_grad
        key_wide, value_wide = key_grad.astype(F32), value_grad.astype(F32)
        head_out[0:2, cols] = key_wide[0:2]
        head_out[2:4, cols] = value_wide[0:2]
        for offset, window in enumerate(delayed(k_ref, cols, 0)):
            part[j, 2 + offset : 3 + offset, :] = jnp.sum(key_wide * window, axis=0, keepdims=True)
        for offset, window in enumerate(delayed(v_ref, cols, 2)):
            part[j, 5 + offset : 6 + offset, :] = jnp.sum(value_wide * window, axis=0, keepdims=True)
        scatter(4, part, parts, j)

    @pl.when(me > 0)
    def _():
        heads.start()

    @pl.when(me == n - 1)
    def _():
        head_in[...] = jnp.zeros(head_in.shape, F32)

    @pl.when(me < slices)
    def _():
        def step(i, carry):
            arrive(4, part, parts, i)
            return carry + parts[i]

        total[me] = lax.fori_loop(0, n, step, jnp.zeros((8, TILE), F32))

        @pl.loop(0, n)
        def _(i):
            @pl.when(i != me)
            def _():
                to_ctx(
                    total.at[me], total.at[me], send_sem.at[5, i], recv_sem.at[5, me], i
                ).start()

    @pl.when(me < n - 1)
    def _():
        heads.wait_recv()

    def advanced(ref, cols, base):
        wide = ref[:, cols].astype(F32)
        first = head_in[base : base + 1, cols]
        second = head_in[base + 1 : base + 2, cols]
        one = jnp.where(row == rows - 1, first, pltpu.roll(wide, rows - 1, 0))
        two = jnp.where(
            row == rows - 1, second,
            jnp.where(row == rows - 2, first, pltpu.roll(wide, rows - 2, 0)),
        )
        return wide, one, two

    @pl.loop(0, slices)
    def _(j):
        cols = columns(j)
        k0, k1, k2 = advanced(kmg, cols, 0)
        kg_ref[:, cols] = (
            k0 * prm_ref[0:1, cols] + k1 * prm_ref[1:2, cols] + k2 * prm_ref[2:3, cols]
        ).astype(BF16)
        v0, v1, v2 = advanced(vmg, cols, 2)
        vg_ref[:, cols] = (
            v0 * prm_ref[3:4, cols] + v1 * prm_ref[4:5, cols] + v2 * prm_ref[5:6, cols]
        ).astype(BF16)

    @pl.loop(0, slices)
    def _(j):
        @pl.when(j != me)
        def _():
            to_ctx(
                total.at[j], total.at[j], send_sem.at[5, 0], recv_sem.at[5, j], j
            ).wait_recv()

        sum_ref[:, columns(j)] = total[j]

    @pl.when(me < n - 1)
    def _():
        tails.wait_send()

    @pl.when(me > 0)
    def _():
        heads.wait_send()

    for i in range(1, n_ch):
        to_ch(i).wait_send()
    sent(0, own, gathered, slices)
    sent(2, own_b, gathered_b, slices)
    sent(4, part, parts, slices)

    @pl.when(me < slices)
    def _():
        sent(1, prefix, incoming, n)
        sent(3, suffix, incoming_b, n)

        @pl.loop(0, n)
        def _(i):
            @pl.when(i != me)
            def _():
                to_ctx(
                    total.at[me], total.at[me], send_sem.at[5, i], recv_sem.at[5, me], i
                ).wait_send()


def local(
    query_proj, key_proj, value_proj, key_taps, value_taps,
    residues, decay_rates, skip_weight, norm_gain, out_grad,
):
    rows, channels = key_proj.shape
    groups, modes = residues.shape
    group_size = channels // groups
    n, n_ch = lax.axis_size("ctx"), lax.axis_size("ch")
    slices = channels // TILE
    assert modes == group_size and slices <= n and rows == 128
    key_spread = jnp.repeat(key_taps.astype(F32).T, group_size, axis=1)
    value_spread = jnp.repeat(value_taps.astype(F32).T, group_size, axis=1)
    params = jnp.concatenate(
        [
            key_spread, value_spread, skip_weight[None], norm_gain[None],
            decay_rates.reshape(1, channels), residues.reshape(1, channels),
            jnp.zeros((6, channels), F32),
        ],
        axis=0,
    )
    rate_rows = jnp.repeat(decay_rates.T, group_size, axis=1)
    positions = jnp.arange(rows).astype(F32)

    def lagged(places):
        return jnp.sum(
            residues[:, :, None] * jnp.exp(-decay_rates[:, :, None] * places[None, None, :]), axis=1
        )

    filt = lagged(positions)
    turned = lagged(jnp.where(positions > 0, rows - positions, 0.0))
    wide = jax.ShapeDtypeStruct((rows, channels), BF16)
    state = lambda count: pltpu.VMEM((count, group_size, TILE), F32)
    whole = lambda kind: pltpu.VMEM((rows, channels), kind)
    vmem = pl.BlockSpec(memory_space=pltpu.VMEM)
    mixed_out, query_grad, key_grad, value_grad, sums = pl.pallas_call(
        functools.partial(body, n, n_ch, slices, float(channels * n_ch), group_size),
        out_shape=(wide, wide, wide, wide, jax.ShapeDtypeStruct((8, channels), F32)),
        in_specs=[vmem] * 8,
        out_specs=(vmem,) * 5,
        scratch_shapes=[
            pltpu.VMEM((4, channels), F32), pltpu.VMEM((4, channels), F32),
            pltpu.VMEM((4, channels), F32), pltpu.VMEM((4, channels), F32),
            whole(BF16), whole(F32), whole(F32), whole(F32), whole(BF16), whole(BF16), whole(BF16),
            state(slices), state(n), state(n), state(slices),
            state(slices), state(n), state(n), state(slices),
            pltpu.VMEM((slices, 8, TILE), F32), pltpu.VMEM((n, 8, TILE), F32),
            pltpu.VMEM((slices, 8, TILE), F32),
            pltpu.VMEM((2, rows, 128), F32), pltpu.VMEM((rows, 128), F32),
            pltpu.VMEM((max(1, n_ch - 1), rows, 128), F32),
            pltpu.SemaphoreType.DMA((2,)), pltpu.SemaphoreType.DMA((2,)),
            pltpu.SemaphoreType.DMA((6, n)), pltpu.SemaphoreType.DMA((6, n)),
            pltpu.SemaphoreType.DMA((max(1, n_ch - 1),)), pltpu.SemaphoreType.DMA((max(1, n_ch - 1),)),
        ],
        compiler_params=pltpu.CompilerParams(
            collective_id=0, has_side_effects=True, vmem_limit_bytes=56 << 20
        ),
        name="hyena",
    )(query_proj, key_proj, value_proj, out_grad, params, rate_rows, filt, turned)
    taps = jnp.sum(sums[2:8].reshape(6, groups, group_size), axis=2)
    return (
        mixed_out, query_grad, key_grad, value_grad,
        taps[0:3].T, taps[3:6].T, sums[0], sums[1],
    )


def solution(mesh):
    wide = P("ctx", "ch")
    placed = (
        wide, wide, wide, P("ch", None), P("ch", None), P("ch", None), P("ch", None),
        P("ch"), P("ch"), wide,
    )
    return jax.shard_map(
        local, mesh=mesh, in_specs=placed,
        out_specs=(wide, wide, wide, wide, P("ch", None), P("ch", None), P("ch"), P("ch")),
        check_vma=False,
    )
```

```python
import functools

import jax
import jax.numpy as jnp
from jax import lax
from jax.experimental import pallas as pl
from jax.experimental.pallas import tpu as pltpu
from jax.sharding import PartitionSpec as P

EPSILON = 1e-06
TILE = 256
CHUNK = 32
HIGHEST = lax.Precision.HIGHEST
F32, BF16 = jnp.float32, jnp.bfloat16


def halves(wide):
    high = wide.astype(BF16)
    return high, (wide - high.astype(F32)).astype(BF16)


def contract_rows(weights, signal):
    return lax.dot_general(weights, signal, (((0,), (0,)), ((), ())), preferred_element_type=F32)


def body(
    n, n_ch, slices, width_all, group_size,
    q_ref, k_ref, v_ref, kt_ref, vt_ref, res_ref, rates_ref, skip_ref, gain_ref, og_ref,
    out_ref, qg_ref, kg_ref, vg_ref, ktg_ref, vtg_ref, skg_ref, gng_ref,
    tail_out, tail_in, head_out, head_in, before, last, taps,
    lag_up, lag_down, filt, turned,
    prod, kmix, vmix, mixed, mgrad,
    own, gathered, prefix, incoming,
    own_b, gathered_b, suffix, incoming_b,
    part, parts, total,
    row_acc, row_out, row_in,
    tail_sem, head_sem, send_sem, recv_sem, ch_send, ch_recv,
):
    me = lax.axis_index("ctx")
    me_ch = lax.axis_index("ch")
    rows = q_ref.shape[0]

    def to_ctx(src, dst, s_sem, r_sem, peer):
        return pltpu.make_async_remote_copy(
            src_ref=src, dst_ref=dst, send_sem=s_sem, recv_sem=r_sem,
            device_id={"ctx": peer}, device_id_type=pl.DeviceIdType.MESH,
        )

    def columns(j):
        return pl.ds(pl.multiple_of(j * TILE, TILE), TILE)

    barrier = pltpu.get_barrier_semaphore()

    @pl.loop(1, n)
    def _(i):
        pl.semaphore_signal(
            barrier, inc=1, device_id={"ctx": lax.rem(me + i, n)},
            device_id_type=pl.DeviceIdType.MESH,
        )

    for i in range(1, n_ch):
        pl.semaphore_signal(
            barrier, inc=1, device_id={"ch": lax.rem(me_ch + i, n_ch)},
            device_id_type=pl.DeviceIdType.MESH,
        )
    tail_out[0:2] = k_ref[rows - 16 : rows].astype(F32)[14:16]
    tail_out[2:4] = v_ref[rows - 16 : rows].astype(F32)[14:16]
    groups_tile = TILE // group_size
    row_wide = lax.broadcasted_iota(jnp.int32, (rows, TILE), 0).astype(F32)
    lane_group = lax.broadcasted_iota(jnp.int32, (CHUNK, TILE), 1) // group_size
    member = (
        lax.broadcasted_iota(jnp.int32, (groups_tile, TILE), 0)
        == lax.broadcasted_iota(jnp.int32, (groups_tile, TILE), 1) // group_size
    )
    member_wide = member.astype(F32)
    repeat_wide = (
        lax.broadcasted_iota(jnp.int32, (group_size, TILE), 0)
        == lax.rem(lax.broadcasted_iota(jnp.int32, (group_size, TILE), 1), group_size)
    ).astype(F32)
    block_mask = (
        lax.broadcasted_iota(jnp.int32, (TILE, TILE), 0) // group_size
        == lax.broadcasted_iota(jnp.int32, (TILE, TILE), 1) // group_size
    )
    tri_row = lax.broadcasted_iota(jnp.int32, (rows, rows), 0)
    tri_col = lax.broadcasted_iota(jnp.int32, (rows, rows), 1)

    def group_rows(j):
        return pl.ds(pl.multiple_of(j * groups_tile, groups_tile), groups_tile)

    def over_channels(table):
        return lax.dot_general(
            table, member_wide, (((0,), (0,)), ((), ())),
            precision=HIGHEST, preferred_element_type=F32,
        )

    def as_line(table):
        wide = jnp.dot(table, repeat_wide, precision=HIGHEST, preferred_element_type=F32)
        return jnp.sum(jnp.where(member, wide, 0.0), axis=0, keepdims=True)

    @pl.loop(0, slices)
    def _(j):
        cols, lines = columns(j), group_rows(j)
        taps[0:3, cols] = over_channels(kt_ref[lines, :].astype(F32))
        taps[3:6, cols] = over_channels(vt_ref[lines, :].astype(F32))
        rate_line = as_line(rates_ref[lines, :])
        a_high, a_low = halves(jnp.where(member, as_line(res_ref[lines, :]), 0.0))
        weights = jnp.concatenate([a_high, a_high, a_low], axis=1)
        for table, filter_rows, lag in (
            (lag_up, filt, row_wide), (lag_down, turned, rows - 1.0 - row_wide)
        ):
            high, low = halves(jnp.exp(-rate_line * lag))
            table[0:rows, cols] = high
            table[rows : 2 * rows, cols] = low
            filter_rows[lines, :] = lax.dot_general(
                weights, jnp.concatenate([high, low, high], axis=1),
                (((1,), (1,)), ((), ())), preferred_element_type=F32,
            )

    pl.semaphore_wait(barrier, n - 1 + n_ch - 1)

    tails = to_ctx(tail_out, tail_in, tail_sem.at[0], tail_sem.at[1], lax.rem(me + 1, n))
    heads = to_ctx(head_out, head_in, head_sem.at[0], head_sem.at[1], lax.rem(me + n - 1, n))

    @pl.when(me < n - 1)
    def _():
        tails.start()

    @pl.when(me == 0)
    def _():
        tail_in[...] = jnp.zeros(tail_in.shape, F32)

    @pl.when(me > 0)
    def _():
        tails.wait_recv()

    before[0, 14:16] = tail_in[0:2]
    before[1, 14:16] = tail_in[2:4]

    def delayed(ref, cols, which, r):
        if r == 0:
            wide = jnp.concatenate([before[which, :, cols], ref[0:CHUNK, cols].astype(F32)], axis=0)
        else:
            wide = ref[r - 16 : r + CHUNK, cols].astype(F32)
        return wide[16 : 16 + CHUNK], wide[15 : 15 + CHUNK], wide[14 : 14 + CHUNK]

    def mix(parts_of, cols, base):
        zero, one, two = parts_of
        return (
            zero * taps[base : base + 1, cols]
            + one * taps[base + 1 : base + 2, cols]
            + two * taps[base + 2 : base + 3, cols]
        )

    def folded(x):
        return jnp.sum(x.reshape(x.shape[0] // 8, 8, TILE), axis=0)

    def modal(table, cols, signal):
        full = contract_rows(table[:, cols], jnp.concatenate([signal, signal], axis=0))
        kept = jnp.where(block_mask, full, 0.0)
        return jnp.sum(kept.reshape(groups_tile, group_size, TILE), axis=0)

    def spread(table, cols, state):
        high, low = table[0:rows, cols], table[rows : 2 * rows, cols]
        s_high, s_low = halves(state)
        zero = jnp.zeros((TILE, TILE), F32)
        big = [
            jnp.where(block_mask, jnp.concatenate([x.astype(F32)] * groups_tile, axis=0), zero)
            .astype(BF16)
            for x in (s_high, s_low)
        ]
        return jnp.dot(
            jnp.concatenate([high, low, high], axis=1),
            jnp.concatenate([big[0], big[0], big[1]], axis=0),
            preferred_element_type=F32,
        )

    def toeplitz(table, shift, j, ref, cols, keep):
        lines = table[group_rows(j), :]
        lhs, rhs = [], []
        for g in range(groups_tile):
            spread_line = jnp.broadcast_to(lines[g : g + 1, :], (rows, rows))
            turned_line = pltpu.roll(spread_line, shift, 1, stride=1, stride_axis=0)
            lhs.append(jnp.where(keep, turned_line, 0.0).astype(BF16))
            for r in range(0, rows, CHUNK):
                wide = ref[r : r + CHUNK, cols].astype(F32)
                rhs.append(jnp.where(lane_group == g, wide, 0.0).astype(BF16))
        return jnp.dot(
            jnp.concatenate(lhs, axis=1), jnp.concatenate(rhs, axis=0),
            preferred_element_type=F32,
        )

    def scatter(phase, source, target, j):
        copy = to_ctx(
            source.at[j], target.at[me], send_sem.at[phase, j], recv_sem.at[phase, me], j
        )

        @pl.when(j != me)
        def _():
            copy.start()

        @pl.when(j == me)
        def _():
            target[me] = source[j]

    def arrive(phase, source, target, i):
        @pl.when(i != me)
        def _():
            to_ctx(
                source.at[0], target.at[i], send_sem.at[phase, 0], recv_sem.at[phase, i], i
            ).wait_recv()

    def sent(phase, source, target, count):
        @pl.loop(0, count)
        def _(j):
            @pl.when(j != me)
            def _():
                to_ctx(
                    source.at[j], target.at[me], send_sem.at[phase, j], recv_sem.at[phase, me], j
                ).wait_send()

    @pl.loop(0, slices)
    def _(i):
        j = lax.rem(me + i, slices)
        cols = columns(j)
        for r in range(0, rows, CHUNK):
            part_rows = slice(r, r + CHUNK)
            key = mix(delayed(k_ref, cols, 0, r), cols, 0)
            value = mix(delayed(v_ref, cols, 1, r), cols, 3)
            kmix[part_rows, cols] = key
            vmix[part_rows, cols] = value
            prod[part_rows, cols] = (key * value).astype(BF16)
        own[j] = modal(lag_down, cols, prod[:, cols])
        scatter(0, own, gathered, j)

    def long_forward(j):
        cols = columns(j)
        mixed[:, cols] = toeplitz(turned, 1, j, prod, cols, tri_row >= tri_col)

    early = slices // 2

    @pl.loop(0, early)
    def _(j):
        long_forward(j)

    @pl.when(me < slices)
    def _():
        rate_here = over_channels(rates_ref[group_rows(me), :])
        fall = jnp.exp(-rate_here * float(rows))
        scale = over_channels(res_ref[group_rows(me), :]) * jnp.exp(-rate_here)

        def step(i, carry):
            prefix[i] = carry * scale
            scatter(1, prefix, incoming, i)
            arrive(0, own, gathered, i)
            return fall * carry + gathered[i]

        lax.fori_loop(0, n, step, jnp.zeros((group_size, TILE), F32))

    @pl.loop(early, slices)
    def _(j):
        long_forward(j)

    row_acc[...] = jnp.zeros(row_acc.shape, F32)

    @pl.loop(0, slices)
    def _(i):
        j = lax.rem(me + i, slices)
        cols = columns(j)
        arrive(1, prefix, incoming, j)
        mixed[:, cols] += spread(lag_up, cols, incoming[j])
        for r in range(0, rows, CHUNK):
            part_rows = slice(r, r + CHUNK)
            full = mixed[part_rows, cols] + skip_ref[0:1, cols] * prod[part_rows, cols].astype(F32)
            mixed[part_rows, cols] = full
            gated = q_ref[part_rows, cols].astype(F32) * full
            squares = gated * gated
            along = gated * gain_ref[0:1, cols] * og_ref[part_rows, cols].astype(F32)
            row_acc[0, part_rows] += squares[:, :128] + squares[:, 128:]
            row_acc[1, part_rows] += along[:, :128] + along[:, 128:]

    lane = lax.broadcasted_iota(jnp.int32, (rows, 128), 1)
    squares = jnp.sum(row_acc[0], axis=1, keepdims=True)
    along = jnp.sum(row_acc[1], axis=1, keepdims=True)
    row_out[...] = jnp.where(lane == 0, squares, along)

    def to_ch(i):
        return pltpu.make_async_remote_copy(
            src_ref=row_out, dst_ref=row_in.at[i - 1], send_sem=ch_send.at[i - 1],
            recv_sem=ch_recv.at[i - 1], device_id={"ch": lax.rem(me_ch + i, n_ch)},
            device_id_type=pl.DeviceIdType.MESH,
        )

    for i in range(1, n_ch):
        to_ch(i).start()
    summed = row_out[...]
    for i in range(1, n_ch):
        to_ch(i).wait_recv()
        summed = summed + row_in[i - 1]
    squares, along = summed[:, 0:1], summed[:, 1:2]
    scaled = lax.rsqrt(squares / width_all + EPSILON)
    pull = scaled * scaled * scaled * along / width_all
    row_acc[0] = jnp.broadcast_to(scaled, (rows, 128))
    row_acc[1] = jnp.broadcast_to(pull, (rows, 128))

    @pl.loop(0, slices)
    def _(i):
        j = lax.rem(me + i, slices)
        cols = columns(j)
        gain = gain_ref[0:1, cols]
        skip_sum = gain_sum = jnp.zeros((8, TILE), F32)
        for r in range(0, rows, CHUNK):
            part_rows = slice(r, r + CHUNK)
            scaled = jnp.concatenate([row_acc[0, part_rows]] * 2, axis=1)
            pull = jnp.concatenate([row_acc[1, part_rows]] * 2, axis=1)
            query = q_ref[part_rows, cols].astype(F32)
            grad = og_ref[part_rows, cols].astype(F32)
            full = mixed[part_rows, cols]
            gated = query * full
            normed = gated * scaled
            out_ref[part_rows, cols] = (normed * gain).astype(BF16)
            gated_grad = scaled * gain * grad - gated * pull
            qg_ref[part_rows, cols] = (gated_grad * full).astype(BF16)
            mixed_grad = (gated_grad * query).astype(BF16)
            mgrad[part_rows, cols] = mixed_grad
            skip_sum += folded(mixed_grad.astype(F32) * prod[part_rows, cols].astype(F32))
            gain_sum += folded(grad * normed)
        part[j, 0:1, :] = jnp.sum(skip_sum, axis=0, keepdims=True)
        part[j, 1:2, :] = jnp.sum(gain_sum, axis=0, keepdims=True)
        own_b[j] = modal(lag_up, cols, mgrad[:, cols])
        scatter(2, own_b, gathered_b, j)

    def long_backward(j):
        cols = columns(j)
        mixed[:, cols] = toeplitz(filt, 0, j, mgrad, cols, tri_row <= tri_col)

    @pl.loop(0, early)
    def _(j):
        long_backward(j)

    @pl.when(me < slices)
    def _():
        rate_here = over_channels(rates_ref[group_rows(me), :])
        fall = jnp.exp(-rate_here * float(rows))
        scale = over_channels(res_ref[group_rows(me), :]) * jnp.exp(-rate_here)

        def step(i, carry):
            place = n - 1 - i
            suffix[place] = carry * scale
            scatter(3, suffix, incoming_b, place)
            arrive(2, own_b, gathered_b, place)
            return fall * carry + gathered_b[place]

        lax.fori_loop(0, n, step, jnp.zeros((group_size, TILE), F32))

    @pl.loop(early, slices)
    def _(j):
        long_backward(j)

    @pl.loop(0, slices)
    def _(i):
        j = lax.rem(me + i, slices)
        cols = columns(j)
        arrive(3, suffix, incoming_b, j)
        mixed[:, cols] += spread(lag_down, cols, incoming_b[j])
        sums = [jnp.zeros((8, TILE), F32)] * 6
        later = [jnp.zeros((8, TILE), F32)] * 2
        for r in reversed(range(0, rows, CHUNK)):
            part_rows = slice(r, r + CHUNK)
            pgrad = (
                mixed[part_rows, cols] + skip_ref[0:1, cols] * mgrad[part_rows, cols].astype(F32)
            )
            for which, (other, signal, target) in enumerate(
                ((vmix, k_ref, kg_ref), (kmix, v_ref, vg_ref))
            ):
                zero = (pgrad * other[part_rows, cols]).astype(BF16).astype(F32)
                wide = jnp.concatenate([zero, later[which]], axis=0)
                shifted = (zero, wide[1 : 1 + CHUNK], wide[2 : 2 + CHUNK])
                later[which] = zero[0:8]
                target[part_rows, cols] = mix(shifted, cols, 3 * which).astype(BF16)
                inside = signal[part_rows, cols].astype(F32)
                for offset in range(3):
                    place = 3 * which + offset
                    sums[place] = sums[place] + folded(shifted[offset] * inside)
                if r == rows - CHUNK:
                    last[which, 0:16, cols] = zero[CHUNK - 16 :]
        for which in range(2):
            first, second = later[which][0:1], later[which][1:2]
            head_out[2 * which : 2 * which + 2, cols] = later[which][0:2]
            older = tail_in[2 * which : 2 * which + 1, cols]
            newer = tail_in[2 * which + 1 : 2 * which + 2, cols]
            edges = (0.0, first * newer, first * older + second * newer)
            for offset in range(3):
                place = 3 * which + offset
                part[j, 2 + place : 3 + place, :] = (
                    jnp.sum(sums[place], axis=0, keepdims=True) + edges[offset]
                )
        scatter(4, part, parts, j)

    @pl.when(me > 0)
    def _():
        heads.start()

    @pl.when(me == n - 1)
    def _():
        head_in[...] = jnp.zeros(head_in.shape, F32)

    @pl.when(me < slices)
    def _():
        def step(i, carry):
            arrive(4, part, parts, i)
            return carry + parts[i]

        total[me] = lax.fori_loop(0, n, step, jnp.zeros((8, TILE), F32))

        @pl.loop(0, n)
        def _(i):
            @pl.when(i != me)
            def _():
                to_ctx(
                    total.at[me], total.at[me], send_sem.at[5, i], recv_sem.at[5, me], i
                ).start()

    @pl.when(me < n - 1)
    def _():
        heads.wait_recv()

    last[0, 16:18] = head_in[0:2]
    last[1, 16:18] = head_in[2:4]

    @pl.loop(0, slices)
    def _(j):
        cols = columns(j)
        for which, target in ((0, kg_ref), (1, vg_ref)):
            wide = last[which, :, cols]
            shifted = (wide[0:16], wide[1:17], wide[2:18])
            target[rows - 16 : rows, cols] = mix(shifted, cols, 3 * which).astype(BF16)

    @pl.loop(0, slices)
    def _(j):
        @pl.when(j != me)
        def _():
            to_ctx(
                total.at[j], total.at[j], send_sem.at[5, 0], recv_sem.at[5, j], j
            ).wait_recv()

        cols, lines = columns(j), group_rows(j)
        here = total[j]
        skg_ref[0:1, cols] = here[0:1]
        gng_ref[0:1, cols] = here[1:2]
        by_group = lax.dot_general(
            member_wide, here, (((1,), (1,)), ((), ())),
            precision=HIGHEST, preferred_element_type=F32,
        )
        ktg_ref[lines, :] = by_group[:, 2:5]
        vtg_ref[lines, :] = by_group[:, 5:8]

    @pl.when(me < n - 1)
    def _():
        tails.wait_send()

    @pl.when(me > 0)
    def _():
        heads.wait_send()

    for i in range(1, n_ch):
        to_ch(i).wait_send()
    sent(0, own, gathered, slices)
    sent(2, own_b, gathered_b, slices)
    sent(4, part, parts, slices)

    @pl.when(me < slices)
    def _():
        sent(1, prefix, incoming, n)
        sent(3, suffix, incoming_b, n)

        @pl.loop(0, n)
        def _(i):
            @pl.when(i != me)
            def _():
                to_ctx(
                    total.at[me], total.at[me], send_sem.at[5, i], recv_sem.at[5, me], i
                ).wait_send()


def local(
    query_proj, key_proj, value_proj, key_taps, value_taps,
    residues, decay_rates, skip_weight, norm_gain, out_grad,
):
    rows, channels = key_proj.shape
    groups, modes = residues.shape
    group_size = channels // groups
    n, n_ch = lax.axis_size("ctx"), lax.axis_size("ch")
    slices = channels // TILE
    assert modes == group_size and slices <= n and rows == 128
    wide = jax.ShapeDtypeStruct((rows, channels), BF16)
    state = lambda count: pltpu.VMEM((count, group_size, TILE), F32)
    whole = lambda kind: pltpu.VMEM((rows, channels), kind)
    vmem = pl.BlockSpec(memory_space=pltpu.VMEM)
    taps_shape = jax.ShapeDtypeStruct(key_taps.shape, F32)
    line_shape = jax.ShapeDtypeStruct((1, channels), F32)
    *results, skip_grad, gain_grad = pl.pallas_call(
        functools.partial(body, n, n_ch, slices, float(channels * n_ch), group_size),
        out_shape=(wide,) * 4 + (taps_shape,) * 2 + (line_shape,) * 2,
        in_specs=[vmem] * 10,
        out_specs=(vmem,) * 8,
        scratch_shapes=[
            pltpu.VMEM((4, channels), F32), pltpu.VMEM((4, channels), F32),
            pltpu.VMEM((4, channels), F32), pltpu.VMEM((4, channels), F32),
            pltpu.VMEM((2, 16, channels), F32), pltpu.VMEM((2, 24, channels), F32),
            pltpu.VMEM((8, channels), F32),
            pltpu.VMEM((2 * rows, channels), BF16), pltpu.VMEM((2 * rows, channels), BF16),
            pltpu.VMEM((groups, rows), F32), pltpu.VMEM((groups, rows), F32),
            whole(BF16), whole(F32), whole(F32), whole(F32), whole(BF16),
            state(slices), state(n), state(n), state(slices),
            state(slices), state(n), state(n), state(slices),
            pltpu.VMEM((slices, 8, TILE), F32), pltpu.VMEM((n, 8, TILE), F32),
            pltpu.VMEM((slices, 8, TILE), F32),
            pltpu.VMEM((2, rows, 128), F32), pltpu.VMEM((rows, 128), F32),
            pltpu.VMEM((max(1, n_ch - 1), rows, 128), F32),
            pltpu.SemaphoreType.DMA((2,)), pltpu.SemaphoreType.DMA((2,)),
            pltpu.SemaphoreType.DMA((6, n)), pltpu.SemaphoreType.DMA((6, n)),
            pltpu.SemaphoreType.DMA((max(1, n_ch - 1),)), pltpu.SemaphoreType.DMA((max(1, n_ch - 1),)),
        ],
        compiler_params=pltpu.CompilerParams(
            collective_id=0, has_side_effects=True, vmem_limit_bytes=56 << 20
        ),
        name="hyena",
    )(
        query_proj, key_proj, value_proj, key_taps, value_taps, residues, decay_rates,
        skip_weight.reshape(1, channels), norm_gain.reshape(1, channels), out_grad,
    )
    return (*results, skip_grad.reshape(channels), gain_grad.reshape(channels))


def solution(mesh):
    wide = P("ctx", "ch")
    placed = (
        wide, wide, wide, P("ch", None), P("ch", None), P("ch", None), P("ch", None),
        P("ch"), P("ch"), wide,
    )
    return jax.shard_map(
        local, mesh=mesh, in_specs=placed,
        out_specs=(wide, wide, wide, wide, P("ch", None), P("ch", None), P("ch"), P("ch")),
        check_vma=False,
    )
```

```python
import functools

import jax
import jax.numpy as jnp
from jax import lax
from jax.experimental import pallas as pl
from jax.experimental.pallas import tpu as pltpu
from jax.sharding import PartitionSpec as P

EPSILON = 1e-06
TILE = 256
CHUNK = 32
HIGHEST = lax.Precision.HIGHEST
F32, BF16 = jnp.float32, jnp.bfloat16


def halves(wide):
    high = wide.astype(BF16)
    return high, (wide - high.astype(F32)).astype(BF16)


def contract_rows(weights, signal):
    return lax.dot_general(weights, signal, (((0,), (0,)), ((), ())), preferred_element_type=F32)


def body(
    n, n_ch, slices, width_all, group_size,
    q_hbm, k_hbm, v_hbm, kt_ref, vt_ref, res_ref, rates_ref, skip_ref, gain_ref, og_hbm,
    out_hbm, qg_hbm, kg_hbm, vg_hbm, ktg_ref, vtg_ref, skg_ref, gng_ref,
    q_ref, k_ref, v_ref, og_ref, out_ref, qg_ref, kg_ref, vg_ref, io_sem, by_group,
    tail_out, tail_in, head_out, head_in, before, last, taps,
    lag_up, lag_down, filt, turned,
    prod, kmix, vmix, mixed, mgrad,
    own, gathered, prefix, incoming,
    own_b, gathered_b, suffix, incoming_b,
    part, parts, total,
    row_acc, row_out, row_in,
    tail_sem, head_sem, send_sem, recv_sem, ch_send, ch_recv,
):
    me = lax.axis_index("ctx")
    me_ch = lax.axis_index("ch")
    rows = q_ref.shape[0]
    load_k, load_v, load_q, load_og = (
        pltpu.make_async_copy(src, dst, io_sem.at[place])
        for place, (src, dst) in enumerate(
            ((k_hbm, k_ref), (v_hbm, v_ref), (q_hbm, q_ref), (og_hbm, og_ref))
        )
    )
    stores = [
        pltpu.make_async_copy(src, dst, io_sem.at[4 + place])
        for place, (src, dst) in enumerate(
            ((out_ref, out_hbm), (qg_ref, qg_hbm), (kg_ref, kg_hbm), (vg_ref, vg_hbm))
        )
    ]

    def to_ctx(src, dst, s_sem, r_sem, peer):
        return pltpu.make_async_remote_copy(
            src_ref=src, dst_ref=dst, send_sem=s_sem, recv_sem=r_sem,
            device_id={"ctx": peer}, device_id_type=pl.DeviceIdType.MESH,
        )

    def columns(j):
        return pl.ds(pl.multiple_of(j * TILE, TILE), TILE)

    barrier = pltpu.get_barrier_semaphore()

    @pl.loop(1, n)
    def _(i):
        pl.semaphore_signal(
            barrier, inc=1, device_id={"ctx": lax.rem(me + i, n)},
            device_id_type=pl.DeviceIdType.MESH,
        )

    for i in range(1, n_ch):
        pl.semaphore_signal(
            barrier, inc=1, device_id={"ch": lax.rem(me_ch + i, n_ch)},
            device_id_type=pl.DeviceIdType.MESH,
        )
    for load in (load_k, load_v, load_q, load_og):
        load.start()
    load_k.wait()
    load_v.wait()
    tail_out[0:2] = k_ref[rows - 16 : rows].astype(F32)[14:16]
    tail_out[2:4] = v_ref[rows - 16 : rows].astype(F32)[14:16]
    groups_tile = TILE // group_size
    row_wide = lax.broadcasted_iota(jnp.int32, (rows, TILE), 0).astype(F32)
    lane_group = lax.broadcasted_iota(jnp.int32, (CHUNK, TILE), 1) // group_size
    member = (
        lax.broadcasted_iota(jnp.int32, (groups_tile, TILE), 0)
        == lax.broadcasted_iota(jnp.int32, (groups_tile, TILE), 1) // group_size
    )
    block_mask = (
        lax.broadcasted_iota(jnp.int32, (TILE, TILE), 0) // group_size
        == lax.broadcasted_iota(jnp.int32, (TILE, TILE), 1) // group_size
    )
    tri_row = lax.broadcasted_iota(jnp.int32, (rows, rows), 0)
    tri_col = lax.broadcasted_iota(jnp.int32, (rows, rows), 1)

    groups = rates_ref.shape[1]
    own_lane = (
        lax.broadcasted_iota(jnp.int32, (group_size, TILE), 0)
        == lax.rem(lax.broadcasted_iota(jnp.int32, (group_size, TILE), 1), group_size)
    )

    def group_rows(j):
        return pl.ds(pl.multiple_of(j * groups_tile, groups_tile), groups_tile)

    def holds(j):
        group = lax.broadcasted_iota(jnp.int32, (groups, TILE), 0)
        channel = lax.broadcasted_iota(jnp.int32, (groups, TILE), 1)
        return (group == j * groups_tile + channel // group_size).astype(F32)

    def over_channels(table, chosen):
        return jnp.dot(table, chosen, precision=HIGHEST, preferred_element_type=F32)

    def as_line(table, chosen):
        return jnp.sum(
            jnp.where(own_lane, over_channels(table, chosen), 0.0), axis=0, keepdims=True
        )

    @pl.loop(0, slices)
    def _(j):
        cols, lines = columns(j), group_rows(j)
        chosen = holds(j)
        chosen_half = chosen.astype(BF16)
        taps[0:3, cols] = jnp.dot(kt_ref[...], chosen_half, preferred_element_type=F32)
        taps[3:6, cols] = jnp.dot(vt_ref[...], chosen_half, preferred_element_type=F32)
        rate_line = as_line(rates_ref[...], chosen)
        a_high, a_low = halves(jnp.where(member, as_line(res_ref[...], chosen), 0.0))
        weights = jnp.concatenate([a_high, a_high, a_low], axis=1)
        for table, filter_rows, lag in (
            (lag_up, filt, row_wide), (lag_down, turned, rows - 1.0 - row_wide)
        ):
            high, low = halves(jnp.exp(-rate_line * lag))
            table[0:rows, cols] = high
            table[rows : 2 * rows, cols] = low
            filter_rows[lines, :] = lax.dot_general(
                weights, jnp.concatenate([high, low, high], axis=1),
                (((1,), (1,)), ((), ())), preferred_element_type=F32,
            )

    pl.semaphore_wait(barrier, n - 1 + n_ch - 1)

    tails = to_ctx(tail_out, tail_in, tail_sem.at[0], tail_sem.at[1], lax.rem(me + 1, n))
    heads = to_ctx(head_out, head_in, head_sem.at[0], head_sem.at[1], lax.rem(me + n - 1, n))

    @pl.when(me < n - 1)
    def _():
        tails.start()

    @pl.when(me == 0)
    def _():
        tail_in[...] = jnp.zeros(tail_in.shape, F32)

    @pl.when(me > 0)
    def _():
        tails.wait_recv()

    before[0, 14:16] = tail_in[0:2]
    before[1, 14:16] = tail_in[2:4]

    def delayed(ref, cols, which, r):
        if r == 0:
            wide = jnp.concatenate([before[which, :, cols], ref[0:CHUNK, cols].astype(F32)], axis=0)
        else:
            wide = ref[r - 16 : r + CHUNK, cols].astype(F32)
        return wide[16 : 16 + CHUNK], wide[15 : 15 + CHUNK], wide[14 : 14 + CHUNK]

    def mix(parts_of, cols, base):
        zero, one, two = parts_of
        return (
            zero * taps[base : base + 1, cols]
            + one * taps[base + 1 : base + 2, cols]
            + two * taps[base + 2 : base + 3, cols]
        )

    def folded(x):
        return jnp.sum(x.reshape(x.shape[0] // 8, 8, TILE), axis=0)

    def modal(table, cols, signal):
        full = contract_rows(table[:, cols], jnp.concatenate([signal, signal], axis=0))
        kept = jnp.where(block_mask, full, 0.0)
        return jnp.sum(kept.reshape(groups_tile, group_size, TILE), axis=0)

    def spread(table, cols, state):
        high, low = table[0:rows, cols], table[rows : 2 * rows, cols]
        s_high, s_low = halves(state)
        zero = jnp.zeros((TILE, TILE), F32)
        big = [
            jnp.where(block_mask, jnp.concatenate([x.astype(F32)] * groups_tile, axis=0), zero)
            .astype(BF16)
            for x in (s_high, s_low)
        ]
        return jnp.dot(
            jnp.concatenate([high, low, high], axis=1),
            jnp.concatenate([big[0], big[0], big[1]], axis=0),
            preferred_element_type=F32,
        )

    def toeplitz(table, shift, j, ref, cols, keep):
        lines = table[group_rows(j), :]
        lhs, rhs = [], []
        for g in range(groups_tile):
            spread_line = jnp.broadcast_to(lines[g : g + 1, :], (rows, rows))
            turned_line = pltpu.roll(spread_line, shift, 1, stride=1, stride_axis=0)
            lhs.append(jnp.where(keep, turned_line, 0.0).astype(BF16))
            for r in range(0, rows, CHUNK):
                wide = ref[r : r + CHUNK, cols].astype(F32)
                rhs.append(jnp.where(lane_group == g, wide, 0.0).astype(BF16))
        return jnp.dot(
            jnp.concatenate(lhs, axis=1), jnp.concatenate(rhs, axis=0),
            preferred_element_type=F32,
        )

    def scatter(phase, source, target, j):
        copy = to_ctx(
            source.at[j], target.at[me], send_sem.at[phase, j], recv_sem.at[phase, me], j
        )

        @pl.when(j != me)
        def _():
            copy.start()

        @pl.when(j == me)
        def _():
            target[me] = source[j]

    def arrive(phase, source, target, i):
        @pl.when(i != me)
        def _():
            to_ctx(
                source.at[0], target.at[i], send_sem.at[phase, 0], recv_sem.at[phase, i], i
            ).wait_recv()

    def sent(phase, source, target, count):
        @pl.loop(0, count)
        def _(j):
            @pl.when(j != me)
            def _():
                to_ctx(
                    source.at[j], target.at[me], send_sem.at[phase, j], recv_sem.at[phase, me], j
                ).wait_send()

    @pl.loop(0, slices)
    def _(i):
        j = lax.rem(me + i, slices)
        cols = columns(j)
        for r in range(0, rows, CHUNK):
            part_rows = slice(r, r + CHUNK)
            key = mix(delayed(k_ref, cols, 0, r), cols, 0)
            value = mix(delayed(v_ref, cols, 1, r), cols, 3)
            kmix[part_rows, cols] = key
            vmix[part_rows, cols] = value
            prod[part_rows, cols] = (key * value).astype(BF16)
        own[j] = modal(lag_down, cols, prod[:, cols])
        scatter(0, own, gathered, j)

    def long_forward(j):
        cols = columns(j)
        mixed[:, cols] = toeplitz(turned, 1, j, prod, cols, tri_row >= tri_col)

    early = slices // 2

    @pl.loop(0, early)
    def _(j):
        long_forward(j)

    @pl.when(me < slices)
    def _():
        chosen = holds(me)
        rate_here = over_channels(rates_ref[...], chosen)
        fall = jnp.exp(-rate_here * float(rows))
        scale = over_channels(res_ref[...], chosen) * jnp.exp(-rate_here)

        def step(i, carry):
            prefix[i] = carry * scale
            scatter(1, prefix, incoming, i)
            arrive(0, own, gathered, i)
            return fall * carry + gathered[i]

        lax.fori_loop(0, n, step, jnp.zeros((group_size, TILE), F32))

    @pl.loop(early, slices)
    def _(j):
        long_forward(j)

    row_acc[...] = jnp.zeros(row_acc.shape, F32)
    load_q.wait()
    load_og.wait()

    @pl.loop(0, slices)
    def _(i):
        j = lax.rem(me + i, slices)
        cols = columns(j)
        arrive(1, prefix, incoming, j)
        mixed[:, cols] += spread(lag_up, cols, incoming[j])
        for r in range(0, rows, CHUNK):
            part_rows = slice(r, r + CHUNK)
            full = mixed[part_rows, cols] + skip_ref[0:1, cols] * prod[part_rows, cols].astype(F32)
            mixed[part_rows, cols] = full
            gated = q_ref[part_rows, cols].astype(F32) * full
            squares = gated * gated
            along = gated * gain_ref[0:1, cols] * og_ref[part_rows, cols].astype(F32)
            row_acc[0, part_rows] += squares[:, :128] + squares[:, 128:]
            row_acc[1, part_rows] += along[:, :128] + along[:, 128:]

    lane = lax.broadcasted_iota(jnp.int32, (rows, 128), 1)
    squares = jnp.sum(row_acc[0], axis=1, keepdims=True)
    along = jnp.sum(row_acc[1], axis=1, keepdims=True)
    row_out[...] = jnp.where(lane == 0, squares, along)

    def to_ch(i):
        return pltpu.make_async_remote_copy(
            src_ref=row_out, dst_ref=row_in.at[i - 1], send_sem=ch_send.at[i - 1],
            recv_sem=ch_recv.at[i - 1], device_id={"ch": lax.rem(me_ch + i, n_ch)},
            device_id_type=pl.DeviceIdType.MESH,
        )

    for i in range(1, n_ch):
        to_ch(i).start()
    summed = row_out[...]
    for i in range(1, n_ch):
        to_ch(i).wait_recv()
        summed = summed + row_in[i - 1]
    squares, along = summed[:, 0:1], summed[:, 1:2]
    scaled = lax.rsqrt(squares / width_all + EPSILON)
    pull = scaled * scaled * scaled * along / width_all
    row_acc[0] = jnp.broadcast_to(scaled, (rows, 128))
    row_acc[1] = jnp.broadcast_to(pull, (rows, 128))

    @pl.loop(0, slices)
    def _(i):
        j = lax.rem(me + i, slices)
        cols = columns(j)
        gain = gain_ref[0:1, cols]
        skip_sum = gain_sum = jnp.zeros((8, TILE), F32)
        for r in range(0, rows, CHUNK):
            part_rows = slice(r, r + CHUNK)
            scaled = jnp.concatenate([row_acc[0, part_rows]] * 2, axis=1)
            pull = jnp.concatenate([row_acc[1, part_rows]] * 2, axis=1)
            query = q_ref[part_rows, cols].astype(F32)
            grad = og_ref[part_rows, cols].astype(F32)
            full = mixed[part_rows, cols]
            gated = query * full
            normed = gated * scaled
            out_ref[part_rows, cols] = (normed * gain).astype(BF16)
            gated_grad = scaled * gain * grad - gated * pull
            qg_ref[part_rows, cols] = (gated_grad * full).astype(BF16)
            mixed_grad = (gated_grad * query).astype(BF16)
            mgrad[part_rows, cols] = mixed_grad
            skip_sum += folded(mixed_grad.astype(F32) * prod[part_rows, cols].astype(F32))
            gain_sum += folded(grad * normed)
        part[j, 0:1, :] = jnp.sum(skip_sum, axis=0, keepdims=True)
        part[j, 1:2, :] = jnp.sum(gain_sum, axis=0, keepdims=True)
        own_b[j] = modal(lag_up, cols, mgrad[:, cols])
        scatter(2, own_b, gathered_b, j)

    stores[0].start()
    stores[1].start()

    def long_backward(j):
        cols = columns(j)
        mixed[:, cols] = toeplitz(filt, 0, j, mgrad, cols, tri_row <= tri_col)

    @pl.loop(0, early)
    def _(j):
        long_backward(j)

    @pl.when(me < slices)
    def _():
        chosen = holds(me)
        rate_here = over_channels(rates_ref[...], chosen)
        fall = jnp.exp(-rate_here * float(rows))
        scale = over_channels(res_ref[...], chosen) * jnp.exp(-rate_here)

        def step(i, carry):
            place = n - 1 - i
            suffix[place] = carry * scale
            scatter(3, suffix, incoming_b, place)
            arrive(2, own_b, gathered_b, place)
            return fall * carry + gathered_b[place]

        lax.fori_loop(0, n, step, jnp.zeros((group_size, TILE), F32))

    @pl.loop(early, slices)
    def _(j):
        long_backward(j)

    @pl.loop(0, slices)
    def _(i):
        j = lax.rem(me + i, slices)
        cols = columns(j)
        arrive(3, suffix, incoming_b, j)
        mixed[:, cols] += spread(lag_down, cols, incoming_b[j])
        sums = [jnp.zeros((8, TILE), F32)] * 6
        later = [jnp.zeros((8, TILE), F32)] * 2
        for r in reversed(range(0, rows, CHUNK)):
            part_rows = slice(r, r + CHUNK)
            pgrad = (
                mixed[part_rows, cols] + skip_ref[0:1, cols] * mgrad[part_rows, cols].astype(F32)
            )
            for which, (other, signal, target) in enumerate(
                ((vmix, k_ref, kg_ref), (kmix, v_ref, vg_ref))
            ):
                zero = (pgrad * other[part_rows, cols]).astype(BF16).astype(F32)
                wide = jnp.concatenate([zero, later[which]], axis=0)
                shifted = (zero, wide[1 : 1 + CHUNK], wide[2 : 2 + CHUNK])
                later[which] = zero[0:8]
                target[part_rows, cols] = mix(shifted, cols, 3 * which).astype(BF16)
                inside = signal[part_rows, cols].astype(F32)
                for offset in range(3):
                    place = 3 * which + offset
                    sums[place] = sums[place] + folded(shifted[offset] * inside)
                if r == rows - CHUNK:
                    last[which, 0:16, cols] = zero[CHUNK - 16 :]
        for which in range(2):
            first, second = later[which][0:1], later[which][1:2]
            head_out[2 * which : 2 * which + 2, cols] = later[which][0:2]
            older = tail_in[2 * which : 2 * which + 1, cols]
            newer = tail_in[2 * which + 1 : 2 * which + 2, cols]
            edges = (0.0, first * newer, first * older + second * newer)
            for offset in range(3):
                place = 3 * which + offset
                part[j, 2 + place : 3 + place, :] = (
                    jnp.sum(sums[place], axis=0, keepdims=True) + edges[offset]
                )
        scatter(4, part, parts, j)

    @pl.when(me > 0)
    def _():
        heads.start()

    @pl.when(me == n - 1)
    def _():
        head_in[...] = jnp.zeros(head_in.shape, F32)

    @pl.when(me < slices)
    def _():
        def step(i, carry):
            arrive(4, part, parts, i)
            return carry + parts[i]

        total[me] = lax.fori_loop(0, n, step, jnp.zeros((8, TILE), F32))

        @pl.loop(0, n)
        def _(i):
            @pl.when(i != me)
            def _():
                to_ctx(
                    total.at[me], total.at[me], send_sem.at[5, i], recv_sem.at[5, me], i
                ).start()

    @pl.when(me < n - 1)
    def _():
        heads.wait_recv()

    last[0, 16:18] = head_in[0:2]
    last[1, 16:18] = head_in[2:4]

    @pl.loop(0, slices)
    def _(j):
        cols = columns(j)
        for which, target in ((0, kg_ref), (1, vg_ref)):
            wide = last[which, :, cols]
            shifted = (wide[0:16], wide[1:17], wide[2:18])
            target[rows - 16 : rows, cols] = mix(shifted, cols, 3 * which).astype(BF16)

    stores[2].start()
    stores[3].start()
    by_group[...] = jnp.zeros(by_group.shape, F32)

    @pl.loop(0, slices)
    def _(j):
        @pl.when(j != me)
        def _():
            to_ctx(
                total.at[j], total.at[j], send_sem.at[5, 0], recv_sem.at[5, j], j
            ).wait_recv()

        cols = columns(j)
        here = total[j]
        skg_ref[0:1, cols] = here[0:1]
        gng_ref[0:1, cols] = here[1:2]
        by_group[...] += lax.dot_general(
            here, holds(j), (((1,), (1,)), ((), ())),
            precision=HIGHEST, preferred_element_type=F32,
        )

    ktg_ref[...] = by_group[2:5]
    vtg_ref[...] = by_group[5:8]
    for store in stores:
        store.wait()

    @pl.when(me < n - 1)
    def _():
        tails.wait_send()

    @pl.when(me > 0)
    def _():
        heads.wait_send()

    for i in range(1, n_ch):
        to_ch(i).wait_send()
    sent(0, own, gathered, slices)
    sent(2, own_b, gathered_b, slices)
    sent(4, part, parts, slices)

    @pl.when(me < slices)
    def _():
        sent(1, prefix, incoming, n)
        sent(3, suffix, incoming_b, n)

        @pl.loop(0, n)
        def _(i):
            @pl.when(i != me)
            def _():
                to_ctx(
                    total.at[me], total.at[me], send_sem.at[5, i], recv_sem.at[5, me], i
                ).wait_send()


def hand_over(*refs):
    count = len(refs) // 2
    sems = refs[-1]
    copies = [
        pltpu.make_async_copy(refs[i], refs[count + i], sems.at[i]) for i in range(count)
    ]
    for copy in copies:
        copy.start()
    for copy in copies:
        copy.wait()


def local(
    query_proj, key_proj, value_proj, key_taps, value_taps,
    residues, decay_rates, skip_weight, norm_gain, out_grad,
):
    rows, channels = key_proj.shape
    groups, modes = residues.shape
    group_size = channels // groups
    n, n_ch = lax.axis_size("ctx"), lax.axis_size("ch")
    slices = channels // TILE
    assert modes == group_size and slices <= n and rows == 128
    wide = jax.ShapeDtypeStruct((rows, channels), BF16)
    state = lambda count: pltpu.VMEM((count, group_size, TILE), F32)
    whole = lambda kind: pltpu.VMEM((rows, channels), kind)
    vmem = pl.BlockSpec(memory_space=pltpu.VMEM)
    anywhere = pl.BlockSpec(memory_space=pl.ANY)
    taps_shape = jax.ShapeDtypeStruct((3, groups), F32)
    line_shape = jax.ShapeDtypeStruct((1, channels), F32)
    shapes = (wide,) * 4 + (taps_shape,) * 2 + (line_shape,) * 2
    results = pl.pallas_call(
        functools.partial(body, n, n_ch, slices, float(channels * n_ch), group_size),
        out_shape=shapes,
        in_specs=[anywhere] * 3 + [vmem] * 6 + [anywhere],
        out_specs=(anywhere,) * 4 + (vmem,) * 4,
        scratch_shapes=[
            *([whole(BF16)] * 8), pltpu.SemaphoreType.DMA((8,)), pltpu.VMEM((8, groups), F32),
            pltpu.VMEM((4, channels), F32), pltpu.VMEM((4, channels), F32),
            pltpu.VMEM((4, channels), F32), pltpu.VMEM((4, channels), F32),
            pltpu.VMEM((2, 16, channels), F32), pltpu.VMEM((2, 24, channels), F32),
            pltpu.VMEM((8, channels), F32),
            pltpu.VMEM((2 * rows, channels), BF16), pltpu.VMEM((2 * rows, channels), BF16),
            pltpu.VMEM((groups, rows), F32), pltpu.VMEM((groups, rows), F32),
            whole(BF16), whole(F32), whole(F32), whole(F32), whole(BF16),
            state(slices), state(n), state(n), state(slices),
            state(slices), state(n), state(n), state(slices),
            pltpu.VMEM((slices, 8, TILE), F32), pltpu.VMEM((n, 8, TILE), F32),
            pltpu.VMEM((slices, 8, TILE), F32),
            pltpu.VMEM((2, rows, 128), F32), pltpu.VMEM((rows, 128), F32),
            pltpu.VMEM((max(1, n_ch - 1), rows, 128), F32),
            pltpu.SemaphoreType.DMA((2,)), pltpu.SemaphoreType.DMA((2,)),
            pltpu.SemaphoreType.DMA((6, n)), pltpu.SemaphoreType.DMA((6, n)),
            pltpu.SemaphoreType.DMA((max(1, n_ch - 1),)), pltpu.SemaphoreType.DMA((max(1, n_ch - 1),)),
        ],
        compiler_params=pltpu.CompilerParams(
            collective_id=0, has_side_effects=True, vmem_limit_bytes=56 << 20
        ),
        name="hyena",
    )(
        query_proj, key_proj, value_proj, key_taps.T, value_taps.T, residues.T, decay_rates.T,
        skip_weight.reshape(1, channels), norm_gain.reshape(1, channels), out_grad,
    )
    results = pl.pallas_call(
        hand_over,
        out_shape=shapes,
        in_specs=[anywhere] * len(shapes),
        out_specs=(anywhere,) * len(shapes),
        scratch_shapes=[pltpu.SemaphoreType.DMA((len(shapes),))],
        name="hand_over",
    )(*results)
    return (
        *results[:4], results[4].T, results[5].T,
        results[6].reshape(channels), results[7].reshape(channels),
    )


def solution(mesh):
    wide = P("ctx", "ch")
    placed = (
        wide, wide, wide, P("ch", None), P("ch", None), P("ch", None), P("ch", None),
        P("ch"), P("ch"), wide,
    )
    return jax.shard_map(
        local, mesh=mesh, in_specs=placed,
        out_specs=(wide, wide, wide, wide, P("ch", None), P("ch", None), P("ch"), P("ch")),
        check_vma=False,
    )
```

```python
import functools

import jax
import jax.numpy as jnp
from jax import lax
from jax.experimental import pallas as pl
from jax.experimental.pallas import tpu as pltpu
from jax.sharding import PartitionSpec as P

EPSILON = 1e-06
TILE = 256
CHUNK = 32
HIGHEST = lax.Precision.HIGHEST
F32, BF16 = jnp.float32, jnp.bfloat16


def halves(wide):
    high = wide.astype(BF16)
    return high, (wide - high.astype(F32)).astype(BF16)


def contract_rows(weights, signal):
    return lax.dot_general(weights, signal, (((0,), (0,)), ((), ())), preferred_element_type=F32)


def body(
    n, n_ch, slices, width_all, group_size,
    q_hbm, k_hbm, v_hbm, kt_ref, vt_ref, res_ref, rates_ref, skip_ref, gain_ref, og_hbm,
    out_hbm, qg_hbm, kg_hbm, vg_hbm, ktg_ref, vtg_ref, skg_ref, gng_ref,
    q_ref, k_ref, v_ref, og_ref, out_ref, qg_ref, kg_ref, vg_ref, io_sem, by_group,
    tail_out, tail_in, head_out, head_in, before, last, taps,
    lag_up, lag_down, filt, turned,
    prod, kmix, vmix, mixed, mgrad,
    own, gathered, prefix, incoming,
    own_b, gathered_b, suffix, incoming_b,
    part, parts, total,
    row_acc, row_out, row_in,
    tail_sem, head_sem, send_sem, recv_sem, ch_send, ch_recv,
):
    me = lax.axis_index("ctx")
    me_ch = lax.axis_index("ch")
    rows = q_ref.shape[0]
    load_k, load_v, load_q, load_og = (
        pltpu.make_async_copy(src, dst, io_sem.at[place])
        for place, (src, dst) in enumerate(
            ((k_hbm, k_ref), (v_hbm, v_ref), (q_hbm, q_ref), (og_hbm, og_ref))
        )
    )
    stores = [
        pltpu.make_async_copy(src, dst, io_sem.at[4 + place])
        for place, (src, dst) in enumerate(
            ((out_ref, out_hbm), (qg_ref, qg_hbm), (kg_ref, kg_hbm), (vg_ref, vg_hbm))
        )
    ]

    def to_ctx(src, dst, s_sem, r_sem, peer):
        return pltpu.make_async_remote_copy(
            src_ref=src, dst_ref=dst, send_sem=s_sem, recv_sem=r_sem,
            device_id={"ctx": peer}, device_id_type=pl.DeviceIdType.MESH,
        )

    def columns(j):
        return pl.ds(pl.multiple_of(j * TILE, TILE), TILE)

    barrier = pltpu.get_barrier_semaphore()

    @pl.loop(1, n)
    def _(i):
        pl.semaphore_signal(
            barrier, inc=1, device_id={"ctx": lax.rem(me + i, n)},
            device_id_type=pl.DeviceIdType.MESH,
        )

    for i in range(1, n_ch):
        pl.semaphore_signal(
            barrier, inc=1, device_id={"ch": lax.rem(me_ch + i, n_ch)},
            device_id_type=pl.DeviceIdType.MESH,
        )
    for load in (load_k, load_v, load_q, load_og):
        load.start()
    load_k.wait()
    load_v.wait()
    tail_out[0:2] = k_ref[rows - 16 : rows].astype(F32)[14:16]
    tail_out[2:4] = v_ref[rows - 16 : rows].astype(F32)[14:16]
    groups_tile = TILE // group_size
    row_wide = lax.broadcasted_iota(jnp.int32, (rows, TILE), 0).astype(F32)
    lane_group = lax.broadcasted_iota(jnp.int32, (CHUNK, TILE), 1) // group_size
    member = (
        lax.broadcasted_iota(jnp.int32, (groups_tile, TILE), 0)
        == lax.broadcasted_iota(jnp.int32, (groups_tile, TILE), 1) // group_size
    )
    block_mask = (
        lax.broadcasted_iota(jnp.int32, (TILE, TILE), 0) // group_size
        == lax.broadcasted_iota(jnp.int32, (TILE, TILE), 1) // group_size
    )
    tri_row = lax.broadcasted_iota(jnp.int32, (rows, rows), 0)
    tri_col = lax.broadcasted_iota(jnp.int32, (rows, rows), 1)

    groups = rates_ref.shape[1]
    own_lane = (
        lax.broadcasted_iota(jnp.int32, (group_size, TILE), 0)
        == lax.rem(lax.broadcasted_iota(jnp.int32, (group_size, TILE), 1), group_size)
    )

    def group_rows(j):
        return pl.ds(pl.multiple_of(j * groups_tile, groups_tile), groups_tile)

    gap = (
        lax.broadcasted_iota(jnp.int32, (groups, TILE), 0)
        - lax.broadcasted_iota(jnp.int32, (groups, TILE), 1) // group_size
    )
    gap_turned = (
        lax.broadcasted_iota(jnp.int32, (TILE, groups), 1)
        - lax.broadcasted_iota(jnp.int32, (TILE, groups), 0) // group_size
    )

    def holds(j):
        return (gap == j * groups_tile).astype(F32)

    def over_channels(table, chosen):
        return jnp.dot(table, chosen, precision=HIGHEST, preferred_element_type=F32)

    def as_line(table, chosen):
        return jnp.sum(
            jnp.where(own_lane, over_channels(table, chosen), 0.0), axis=0, keepdims=True
        )

    @pl.loop(0, slices)
    def _(j):
        cols, lines = columns(j), group_rows(j)
        chosen = holds(j)
        chosen_half = chosen.astype(BF16)
        taps[0:3, cols] = jnp.dot(kt_ref[...], chosen_half, preferred_element_type=F32)
        taps[3:6, cols] = jnp.dot(vt_ref[...], chosen_half, preferred_element_type=F32)
        rate_line = as_line(rates_ref[...], chosen)
        a_high, a_low = halves(jnp.where(member, as_line(res_ref[...], chosen), 0.0))
        weights = jnp.concatenate([a_high, a_high, a_low], axis=1)
        for table, filter_rows, lag in (
            (lag_up, filt, row_wide), (lag_down, turned, rows - 1.0 - row_wide)
        ):
            high, low = halves(jnp.exp(-rate_line * lag))
            table[0:rows, cols] = high
            table[rows : 2 * rows, cols] = low
            filter_rows[lines, :] = lax.dot_general(
                weights, jnp.concatenate([high, low, high], axis=1),
                (((1,), (1,)), ((), ())), preferred_element_type=F32,
            )

    pl.semaphore_wait(barrier, n - 1 + n_ch - 1)

    tails = to_ctx(tail_out, tail_in, tail_sem.at[0], tail_sem.at[1], lax.rem(me + 1, n))
    heads = to_ctx(head_out, head_in, head_sem.at[0], head_sem.at[1], lax.rem(me + n - 1, n))

    @pl.when(me < n - 1)
    def _():
        tails.start()

    @pl.when(me == 0)
    def _():
        tail_in[...] = jnp.zeros(tail_in.shape, F32)

    @pl.when(me > 0)
    def _():
        tails.wait_recv()

    before[0, 14:16] = tail_in[0:2]
    before[1, 14:16] = tail_in[2:4]

    def delayed(ref, cols, which, r):
        if r == 0:
            wide = jnp.concatenate([before[which, :, cols], ref[0:CHUNK, cols].astype(F32)], axis=0)
        else:
            wide = ref[r - 16 : r + CHUNK, cols].astype(F32)
        return wide[16 : 16 + CHUNK], wide[15 : 15 + CHUNK], wide[14 : 14 + CHUNK]

    def mix(parts_of, cols, base):
        zero, one, two = parts_of
        return (
            zero * taps[base : base + 1, cols]
            + one * taps[base + 1 : base + 2, cols]
            + two * taps[base + 2 : base + 3, cols]
        )

    def folded(x):
        return jnp.sum(x.reshape(x.shape[0] // 8, 8, TILE), axis=0)

    def modal(table, cols, signal):
        full = contract_rows(table[:, cols], jnp.concatenate([signal, signal], axis=0))
        kept = jnp.where(block_mask, full, 0.0)
        return jnp.sum(kept.reshape(groups_tile, group_size, TILE), axis=0)

    def spread(table, cols, state):
        high, low = table[0:rows, cols], table[rows : 2 * rows, cols]
        s_high, s_low = halves(state)
        zero = jnp.zeros((TILE, TILE), F32)
        big = [
            jnp.where(block_mask, jnp.concatenate([x.astype(F32)] * groups_tile, axis=0), zero)
            .astype(BF16)
            for x in (s_high, s_low)
        ]
        return jnp.dot(
            jnp.concatenate([high, low, high], axis=1),
            jnp.concatenate([big[0], big[0], big[1]], axis=0),
            preferred_element_type=F32,
        )

    def toeplitz(table, shift, j, ref, cols, keep):
        lines = table[group_rows(j), :]
        lhs, rhs = [], []
        for g in range(groups_tile):
            spread_line = jnp.broadcast_to(lines[g : g + 1, :], (rows, rows))
            turned_line = pltpu.roll(spread_line, shift, 1, stride=1, stride_axis=0)
            lhs.append(jnp.where(keep, turned_line, 0.0).astype(BF16))
            for r in range(0, rows, CHUNK):
                wide = ref[r : r + CHUNK, cols].astype(F32)
                rhs.append(jnp.where(lane_group == g, wide, 0.0).astype(BF16))
        return jnp.dot(
            jnp.concatenate(lhs, axis=1), jnp.concatenate(rhs, axis=0),
            preferred_element_type=F32,
        )

    def scatter(phase, source, target, j):
        copy = to_ctx(
            source.at[j], target.at[me], send_sem.at[phase, j], recv_sem.at[phase, me], j
        )

        @pl.when(j != me)
        def _():
            copy.start()

        @pl.when(j == me)
        def _():
            target[me] = source[j]

    def arrive(phase, source, target, i):
        @pl.when(i != me)
        def _():
            to_ctx(
                source.at[0], target.at[i], send_sem.at[phase, 0], recv_sem.at[phase, i], i
            ).wait_recv()

    def sent(phase, source, target, count):
        @pl.loop(0, count)
        def _(j):
            @pl.when(j != me)
            def _():
                to_ctx(
                    source.at[j], target.at[me], send_sem.at[phase, j], recv_sem.at[phase, me], j
                ).wait_send()

    @pl.loop(0, slices)
    def _(i):
        j = lax.rem(me + i, slices)
        cols = columns(j)
        for r in range(0, rows, CHUNK):
            part_rows = slice(r, r + CHUNK)
            key = mix(delayed(k_ref, cols, 0, r), cols, 0)
            value = mix(delayed(v_ref, cols, 1, r), cols, 3)
            kmix[part_rows, cols] = key
            vmix[part_rows, cols] = value
            prod[part_rows, cols] = (key * value).astype(BF16)
        own[j] = modal(lag_down, cols, prod[:, cols])
        scatter(0, own, gathered, j)

    def long_forward(j):
        cols = columns(j)
        mixed[:, cols] = toeplitz(turned, 1, j, prod, cols, tri_row >= tri_col)

    early = slices // 2

    @pl.loop(0, early)
    def _(j):
        long_forward(j)

    @pl.when(me < slices)
    def _():
        chosen = holds(me)
        rate_here = over_channels(rates_ref[...], chosen)
        fall = jnp.exp(-rate_here * float(rows))
        scale = over_channels(res_ref[...], chosen) * jnp.exp(-rate_here)

        def step(i, carry):
            prefix[i] = carry * scale
            scatter(1, prefix, incoming, i)
            arrive(0, own, gathered, i)
            return fall * carry + gathered[i]

        lax.fori_loop(0, n, step, jnp.zeros((group_size, TILE), F32))

    @pl.loop(early, slices)
    def _(j):
        long_forward(j)

    row_acc[...] = jnp.zeros(row_acc.shape, F32)
    load_q.wait()
    load_og.wait()

    @pl.loop(0, slices)
    def _(i):
        j = lax.rem(me + i, slices)
        cols = columns(j)
        arrive(1, prefix, incoming, j)
        mixed[:, cols] += spread(lag_up, cols, incoming[j])
        for r in range(0, rows, CHUNK):
            part_rows = slice(r, r + CHUNK)
            full = mixed[part_rows, cols] + skip_ref[0:1, cols] * prod[part_rows, cols].astype(F32)
            mixed[part_rows, cols] = full
            gated = q_ref[part_rows, cols].astype(F32) * full
            squares = gated * gated
            along = gated * gain_ref[0:1, cols] * og_ref[part_rows, cols].astype(F32)
            row_acc[0, part_rows] += squares[:, :128] + squares[:, 128:]
            row_acc[1, part_rows] += along[:, :128] + along[:, 128:]

    lane = lax.broadcasted_iota(jnp.int32, (rows, 128), 1)
    squares = jnp.sum(row_acc[0], axis=1, keepdims=True)
    along = jnp.sum(row_acc[1], axis=1, keepdims=True)
    row_out[...] = jnp.where(lane == 0, squares, along)

    def to_ch(i):
        return pltpu.make_async_remote_copy(
            src_ref=row_out, dst_ref=row_in.at[i - 1], send_sem=ch_send.at[i - 1],
            recv_sem=ch_recv.at[i - 1], device_id={"ch": lax.rem(me_ch + i, n_ch)},
            device_id_type=pl.DeviceIdType.MESH,
        )

    for i in range(1, n_ch):
        to_ch(i).start()
    summed = row_out[...]
    for i in range(1, n_ch):
        to_ch(i).wait_recv()
        summed = summed + row_in[i - 1]
    squares, along = summed[:, 0:1], summed[:, 1:2]
    scaled = lax.rsqrt(squares / width_all + EPSILON)
    pull = scaled * scaled * scaled * along / width_all
    row_acc[0] = jnp.broadcast_to(scaled, (rows, 128))
    row_acc[1] = jnp.broadcast_to(pull, (rows, 128))

    @pl.loop(0, slices)
    def _(i):
        j = lax.rem(me + i, slices)
        cols = columns(j)
        gain = gain_ref[0:1, cols]
        skip_sum = gain_sum = jnp.zeros((8, TILE), F32)
        for r in range(0, rows, CHUNK):
            part_rows = slice(r, r + CHUNK)
            scaled = jnp.concatenate([row_acc[0, part_rows]] * 2, axis=1)
            pull = jnp.concatenate([row_acc[1, part_rows]] * 2, axis=1)
            query = q_ref[part_rows, cols].astype(F32)
            grad = og_ref[part_rows, cols].astype(F32)
            full = mixed[part_rows, cols]
            gated = query * full
            normed = gated * scaled
            out_ref[part_rows, cols] = (normed * gain).astype(BF16)
            gated_grad = scaled * gain * grad - gated * pull
            qg_ref[part_rows, cols] = (gated_grad * full).astype(BF16)
            mixed_grad = (gated_grad * query).astype(BF16)
            mgrad[part_rows, cols] = mixed_grad
            skip_sum += folded(mixed_grad.astype(F32) * prod[part_rows, cols].astype(F32))
            gain_sum += folded(grad * normed)
        part[j, 0:1, :] = jnp.sum(skip_sum, axis=0, keepdims=True)
        part[j, 1:2, :] = jnp.sum(gain_sum, axis=0, keepdims=True)
        own_b[j] = modal(lag_up, cols, mgrad[:, cols])
        scatter(2, own_b, gathered_b, j)

    stores[0].start()
    stores[1].start()

    def long_backward(j):
        cols = columns(j)
        mixed[:, cols] = toeplitz(filt, 0, j, mgrad, cols, tri_row <= tri_col)

    @pl.loop(0, early)
    def _(j):
        long_backward(j)

    @pl.when(me < slices)
    def _():
        chosen = holds(me)
        rate_here = over_channels(rates_ref[...], chosen)
        fall = jnp.exp(-rate_here * float(rows))
        scale = over_channels(res_ref[...], chosen) * jnp.exp(-rate_here)

        def step(i, carry):
            place = n - 1 - i
            suffix[place] = carry * scale
            scatter(3, suffix, incoming_b, place)
            arrive(2, own_b, gathered_b, place)
            return fall * carry + gathered_b[place]

        lax.fori_loop(0, n, step, jnp.zeros((group_size, TILE), F32))

    @pl.loop(early, slices)
    def _(j):
        long_backward(j)

    @pl.loop(0, slices)
    def _(i):
        j = lax.rem(me + i, slices)
        cols = columns(j)
        arrive(3, suffix, incoming_b, j)
        mixed[:, cols] += spread(lag_down, cols, incoming_b[j])
        sums = [jnp.zeros((8, TILE), F32)] * 6
        later = [jnp.zeros((8, TILE), F32)] * 2
        for r in reversed(range(0, rows, CHUNK)):
            part_rows = slice(r, r + CHUNK)
            pgrad = (
                mixed[part_rows, cols] + skip_ref[0:1, cols] * mgrad[part_rows, cols].astype(F32)
            )
            for which, (other, signal, target) in enumerate(
                ((vmix, k_ref, kg_ref), (kmix, v_ref, vg_ref))
            ):
                zero = (pgrad * other[part_rows, cols]).astype(BF16).astype(F32)
                wide = jnp.concatenate([zero, later[which]], axis=0)
                shifted = (zero, wide[1 : 1 + CHUNK], wide[2 : 2 + CHUNK])
                later[which] = zero[0:8]
                target[part_rows, cols] = mix(shifted, cols, 3 * which).astype(BF16)
                inside = signal[part_rows, cols].astype(F32)
                for offset in range(3):
                    place = 3 * which + offset
                    sums[place] = sums[place] + folded(shifted[offset] * inside)
                if r == rows - CHUNK:
                    last[which, 0:16, cols] = zero[CHUNK - 16 :]
        for which in range(2):
            first, second = later[which][0:1], later[which][1:2]
            head_out[2 * which : 2 * which + 2, cols] = later[which][0:2]
            older = tail_in[2 * which : 2 * which + 1, cols]
            newer = tail_in[2 * which + 1 : 2 * which + 2, cols]
            edges = (0.0, first * newer, first * older + second * newer)
            for offset in range(3):
                place = 3 * which + offset
                part[j, 2 + place : 3 + place, :] = (
                    jnp.sum(sums[place], axis=0, keepdims=True) + edges[offset]
                )
        scatter(4, part, parts, j)

    @pl.when(me > 0)
    def _():
        heads.start()

    @pl.when(me == n - 1)
    def _():
        head_in[...] = jnp.zeros(head_in.shape, F32)

    @pl.when(me < slices)
    def _():
        def step(i, carry):
            arrive(4, part, parts, i)
            return carry + parts[i]

        total[me] = lax.fori_loop(0, n, step, jnp.zeros((8, TILE), F32))

        @pl.loop(0, n)
        def _(i):
            @pl.when(i != me)
            def _():
                to_ctx(
                    total.at[me], total.at[me], send_sem.at[5, i], recv_sem.at[5, me], i
                ).start()

    @pl.when(me < n - 1)
    def _():
        heads.wait_recv()

    last[0, 16:18] = head_in[0:2]
    last[1, 16:18] = head_in[2:4]

    @pl.loop(0, slices)
    def _(j):
        cols = columns(j)
        for which, target in ((0, kg_ref), (1, vg_ref)):
            wide = last[which, :, cols]
            shifted = (wide[0:16], wide[1:17], wide[2:18])
            target[rows - 16 : rows, cols] = mix(shifted, cols, 3 * which).astype(BF16)

    stores[2].start()
    stores[3].start()
    by_group[...] = jnp.zeros(by_group.shape, F32)

    @pl.loop(0, slices)
    def _(j):
        @pl.when(j != me)
        def _():
            to_ctx(
                total.at[j], total.at[j], send_sem.at[5, 0], recv_sem.at[5, j], j
            ).wait_recv()

        cols = columns(j)
        here = total[j]
        skg_ref[0:1, cols] = here[0:1]
        gng_ref[0:1, cols] = here[1:2]
        by_group[...] += jnp.dot(
            here, (gap_turned == j * groups_tile).astype(F32),
            precision=HIGHEST, preferred_element_type=F32,
        )

    ktg_ref[...] = by_group[2:5]
    vtg_ref[...] = by_group[5:8]
    for store in stores:
        store.wait()

    @pl.when(me < n - 1)
    def _():
        tails.wait_send()

    @pl.when(me > 0)
    def _():
        heads.wait_send()

    for i in range(1, n_ch):
        to_ch(i).wait_send()
    sent(0, own, gathered, slices)
    sent(2, own_b, gathered_b, slices)
    sent(4, part, parts, slices)

    @pl.when(me < slices)
    def _():
        sent(1, prefix, incoming, n)
        sent(3, suffix, incoming_b, n)

        @pl.loop(0, n)
        def _(i):
            @pl.when(i != me)
            def _():
                to_ctx(
                    total.at[me], total.at[me], send_sem.at[5, i], recv_sem.at[5, me], i
                ).wait_send()


def hand_over(count, *refs):
    sources, targets, staged = refs[:count], refs[count : 2 * count], refs[2 * count : 3 * count]
    sems = refs[-1]
    loads = [
        pltpu.make_async_copy(sources[i], staged[i], sems.at[i]) for i in range(count)
    ]
    stores = [
        pltpu.make_async_copy(staged[i], targets[i], sems.at[count + i]) for i in range(count)
    ]
    for load in loads:
        load.start()
    for load, store in zip(loads, stores):
        load.wait()
        store.start()
    for store in stores:
        store.wait()


def local(
    query_proj, key_proj, value_proj, key_taps, value_taps,
    residues, decay_rates, skip_weight, norm_gain, out_grad,
):
    rows, channels = key_proj.shape
    groups, modes = residues.shape
    group_size = channels // groups
    n, n_ch = lax.axis_size("ctx"), lax.axis_size("ch")
    slices = channels // TILE
    assert modes == group_size and slices <= n and rows == 128
    wide = jax.ShapeDtypeStruct((rows, channels), BF16)
    state = lambda count: pltpu.VMEM((count, group_size, TILE), F32)
    whole = lambda kind: pltpu.VMEM((rows, channels), kind)
    vmem = pl.BlockSpec(memory_space=pltpu.VMEM)
    anywhere = pl.BlockSpec(memory_space=pl.ANY)
    taps_shape = jax.ShapeDtypeStruct((3, groups), F32)
    line_shape = jax.ShapeDtypeStruct((1, channels), F32)
    shapes = (wide,) * 4 + (taps_shape,) * 2 + (line_shape,) * 2
    results = pl.pallas_call(
        functools.partial(body, n, n_ch, slices, float(channels * n_ch), group_size),
        out_shape=shapes,
        in_specs=[anywhere] * 3 + [vmem] * 6 + [anywhere],
        out_specs=(anywhere,) * 4 + (vmem,) * 4,
        scratch_shapes=[
            *([whole(BF16)] * 8), pltpu.SemaphoreType.DMA((8,)), pltpu.VMEM((8, groups), F32),
            pltpu.VMEM((4, channels), F32), pltpu.VMEM((4, channels), F32),
            pltpu.VMEM((4, channels), F32), pltpu.VMEM((4, channels), F32),
            pltpu.VMEM((2, 16, channels), F32), pltpu.VMEM((2, 24, channels), F32),
            pltpu.VMEM((8, channels), F32),
            pltpu.VMEM((2 * rows, channels), BF16), pltpu.VMEM((2 * rows, channels), BF16),
            pltpu.VMEM((groups, rows), F32), pltpu.VMEM((groups, rows), F32),
            whole(BF16), whole(F32), whole(F32), whole(F32), whole(BF16),
            state(slices), state(n), state(n), state(slices),
            state(slices), state(n), state(n), state(slices),
            pltpu.VMEM((slices, 8, TILE), F32), pltpu.VMEM((n, 8, TILE), F32),
            pltpu.VMEM((slices, 8, TILE), F32),
            pltpu.VMEM((2, rows, 128), F32), pltpu.VMEM((rows, 128), F32),
            pltpu.VMEM((max(1, n_ch - 1), rows, 128), F32),
            pltpu.SemaphoreType.DMA((2,)), pltpu.SemaphoreType.DMA((2,)),
            pltpu.SemaphoreType.DMA((6, n)), pltpu.SemaphoreType.DMA((6, n)),
            pltpu.SemaphoreType.DMA((max(1, n_ch - 1),)), pltpu.SemaphoreType.DMA((max(1, n_ch - 1),)),
        ],
        compiler_params=pltpu.CompilerParams(
            collective_id=0, has_side_effects=True, vmem_limit_bytes=56 << 20
        ),
        name="hyena",
    )(
        query_proj, key_proj, value_proj, key_taps.T, value_taps.T, residues.T, decay_rates.T,
        skip_weight.reshape(1, channels), norm_gain.reshape(1, channels), out_grad,
    )
    results = pl.pallas_call(
        functools.partial(hand_over, len(shapes)),
        out_shape=shapes,
        in_specs=[anywhere] * len(shapes),
        out_specs=(anywhere,) * len(shapes),
        scratch_shapes=[
            *(pltpu.VMEM(shape.shape, shape.dtype) for shape in shapes),
            pltpu.SemaphoreType.DMA((2 * len(shapes),)),
        ],
        name="hand_over",
    )(*results)
    return (
        *results[:4], results[4].T, results[5].T,
        results[6].reshape(channels), results[7].reshape(channels),
    )


def solution(mesh):
    wide = P("ctx", "ch")
    placed = (
        wide, wide, wide, P("ch", None), P("ch", None), P("ch", None), P("ch", None),
        P("ch"), P("ch"), wide,
    )
    return jax.shard_map(
        local, mesh=mesh, in_specs=placed,
        out_specs=(wide, wide, wide, wide, P("ch", None), P("ch", None), P("ch"), P("ch")),
        check_vma=False,
    )
```
